512 devices in a mesh: ctx: 64 (over z, y), head: 8 (over x, core).
Axes of the slice: x: 4, y: 4, z: 16, core: 2. Of those that a mesh axis runs over, the one named last changes fastest.
Arguments:
- queries: bfloat16 [32768, 1024], P('ctx', 'head'), may hold values from -6 to 6
- keys: bfloat16 [32768, 1024], P('ctx', 'head'), may hold values from -6 to 6
- values: bfloat16 [32768, 1024], P('ctx', 'head'), may hold values from -6 to 6
- out_grad: bfloat16 [32768, 1024], P('ctx', 'head'), may hold values from -12 to 12
- cluster_ids: int32 [512], P('ctx'), may hold values from 0 to 255, as said below
Outputs:
- queries_grad: bfloat16 [32768, 1024], P('ctx', 'head')
- keys_grad: bfloat16 [32768, 1024], P('ctx', 'head')
- values_grad: bfloat16 [32768, 1024], P('ctx', 'head')
- centroids: float32 [256, 128], P('ctx')
The draws below stay inside these ranges and needn't reach their ends.
Inputs may be any that keep to these rules, and one draw needn't show every extreme that they name: `cluster_ids`: cluster c is owned by index c // 4 of ctx. The 8 blocks of one index of ctx go 1 at a time: exactly 1 of them to each of 8 owners and none to the others; every owner receives exactly 8 blocks.
All inputs are finite; a program needn't handle non-finite values.
Results may differ from the reference program's by a relative error of at most 0.012.
The reference program's roundings to bfloat16 on the way (of `probs_low` and `dscore`) count: a program that leaves them out, or rounds other values in their place, can miss the bound.
Values may be sent and summed in bfloat16 or wider, within the bound.
A program may use at most 64 MiB of HBM per device.

```python
import math
import jax
import jax.numpy as jnp
from jax import lax

HDIM = 128
HEADS = 8
BLK = 64
BLK_DEV = 8
CLUS_DEV = 4
SLOTS = 1
TOKENS = 32768
NBLK = 512
CLUSTERS = 256
HD = 1024
N_CTX = 64


def column_scale(key):
    return jnp.exp(jax.random.uniform(key, (1, HD), jnp.float32, math.log(0.4), math.log(2.5)))


def draw_queries(key, part):
    key_main, key_column = jax.random.split(jax.random.fold_in(key, 1))
    column = column_scale(key_column)
    base = jax.random.truncated_normal(key_main, -2.4, 2.4, (TOKENS, HD), jnp.float32) * 0.9 * column
    return base.astype(jnp.bfloat16)


def draw_keys(key, part):
    key_main, key_column = jax.random.split(jax.random.fold_in(key, 2), 2)
    column = column_scale(key_column)
    heads_rise = (3.0 ** ((jnp.arange(HD) // HDIM).astype(jnp.float32) / max(HEADS - 1, 1)))[None, :]
    base = jax.random.truncated_normal(key_main, -1.6, 1.6, (TOKENS, HD), jnp.float32) * 0.5 * column * heads_rise
    return base.astype(jnp.bfloat16)


def draw_cluster_ids(key, part):
    sources = NBLK // BLK_DEV
    pairs = BLK_DEV // SLOTS
    first, second, third, fourth = jax.random.split(jax.random.fold_in(key, 3), 4)
    shuffled = jax.random.permutation(first, sources)
    order_score = jnp.where(jnp.arange(sources) == sources // 2, -1, shuffled)
    order_score = jnp.where(jnp.arange(sources) == 1, -2, order_score)
    order_score = jnp.where(jnp.arange(sources) == sources - 1, -3, order_score)
    offsets = jnp.argsort(order_score)[:pairs].astype(jnp.int32)
    ranking = jax.random.randint(second, (sources, BLK_DEV), 0, 1 << 20) * BLK_DEV + jnp.arange(BLK_DEV)[None, :]
    placing = jnp.argsort(jnp.argsort(ranking, axis=1), axis=1)
    pair_of = placing // SLOTS
    owner_dev = (jnp.arange(sources)[:, None] + offsets[pair_of]) % sources
    within = jnp.minimum(jax.random.randint(third, (sources, BLK_DEV), 0, CLUS_DEV), jax.random.randint(fourth, (sources, BLK_DEV), 0, CLUS_DEV))
    return (owner_dev * CLUS_DEV + within).reshape(-1).astype(jnp.int32)


def level_of(key, dims, shards, smallest, largest):
    loudness, own = 1.0, jax.random.fold_in(key, 6)
    for dim, shards_of in shards:
        steps = jnp.exp(jax.random.uniform(jax.random.fold_in(own, dim), (shards_of,), jnp.float32, smallest / len(shards), largest / len(shards)))
        loudness = loudness * jnp.repeat(steps, dims[dim] // shards_of).reshape([-1 if axis == dim else 1 for axis in range(len(dims))])
    return loudness


def scatter_about(rng, dims, spread, most, pieces=(), held_as=jnp.bfloat16):
    result = spread * jax.random.normal(rng, dims, jnp.float32)
    if pieces:
        result = result * level_of(rng, dims, pieces, -0.22, 0.18)
    return jnp.clip(result, -most, most).astype(held_as)


def setup_inputs(seed: int = 0) -> dict:
    splits = jax.random.split(jax.random.key(seed), 6)
    queries = draw_queries(jax.random.fold_in(splits[5], 71), 0)
    keys = draw_keys(jax.random.fold_in(splits[5], 71), 0)
    values = scatter_about(splits[2], (TOKENS, HD), 1.0, 6.0, ((0, 64), (1, 8)))
    out_grad = scatter_about(splits[3], (TOKENS, HD), 2.0, 12.0, ((0, 64), (1, 8)))
    cluster_ids = draw_cluster_ids(jax.random.fold_in(splits[5], 71), 0)
    return {"queries": queries, "keys": keys, "values": values, "out_grad": out_grad, "cluster_ids": cluster_ids}


def head_grads(q_rows, k_rows, v_rows, g_rows, allowed, score_scale):
    scores = jnp.dot(q_rows, k_rows.T, preferred_element_type=jnp.float32) * score_scale
    scores = jnp.where(allowed, scores, -jnp.inf)
    row_peak = lax.optimization_barrier(jnp.max(scores, axis=1, keepdims=True))
    exponent = jnp.exp(scores - row_peak)
    probs = exponent / lax.optimization_barrier(jnp.sum(exponent, axis=1, keepdims=True))
    probs_low = probs.astype(jnp.bfloat16)
    attn_out = jnp.dot(probs_low, v_rows, preferred_element_type=jnp.float32)
    delta_row = lax.optimization_barrier(jnp.sum(g_rows.astype(jnp.float32) * attn_out, axis=1, keepdims=True))
    values_part = jnp.dot(probs_low.T, g_rows, preferred_element_type=jnp.float32)
    dprob = jnp.dot(g_rows, v_rows.T, preferred_element_type=jnp.float32)
    dscore = (probs * (dprob - delta_row)).astype(jnp.bfloat16)
    queries_part = jnp.dot(dscore, k_rows, preferred_element_type=jnp.float32) * score_scale
    keys_part = jnp.dot(dscore.T, q_rows, preferred_element_type=jnp.float32) * score_scale
    return (queries_part, keys_part, values_part)

def reference(queries, keys, values, out_grad, cluster_ids):
    score_scale = 1.0 / math.sqrt(HDIM)
    row_total = BLK * BLK_DEV
    owner_dev = cluster_ids // CLUS_DEV
    positions = jnp.arange(row_total, dtype=jnp.int32)
    causal = positions[None, :] <= positions[:, None]

    def per_owner(carry, which):
        grads_q, grads_k, grads_v = carry
        chosen = jnp.argsort(jnp.where(owner_dev == which, 0, 1), stable=True)[:BLK_DEV].astype(jnp.int32)
        row_index = (chosen[:, None] * BLK + jnp.arange(BLK, dtype=jnp.int32)[None, :]).reshape(-1)
        row_cluster = jnp.repeat(cluster_ids[chosen], BLK)
        allowed = (row_cluster[:, None] == row_cluster[None, :]) & causal
        q_all = queries[row_index]
        k_all = keys[row_index]
        v_all = values[row_index]
        g_all = out_grad[row_index]
        list_q, list_k, list_v = ([], [], [])
        for head_index in range(HEADS):
            lower = head_index * HDIM
            upper = lower + HDIM
            part_q, part_k, part_v = head_grads(q_all[:, lower:upper], k_all[:, lower:upper], v_all[:, lower:upper], g_all[:, lower:upper], allowed, score_scale)
            list_q.append(part_q)
            list_k.append(part_k)
            list_v.append(part_v)
        grads_q = grads_q.at[row_index].set(jnp.concatenate(list_q, axis=1).astype(jnp.bfloat16))
        grads_k = grads_k.at[row_index].set(jnp.concatenate(list_k, axis=1).astype(jnp.bfloat16))
        grads_v = grads_v.at[row_index].set(jnp.concatenate(list_v, axis=1).astype(jnp.bfloat16))
        return ((grads_q, grads_k, grads_v), None)
    zero_grads = jnp.zeros((TOKENS, HD), jnp.bfloat16)
    (grads_q, grads_k, grads_v), _ = lax.scan(per_owner, (zero_grads, zero_grads, zero_grads), jnp.arange(N_CTX, dtype=jnp.int32))
    key_heads = keys.astype(jnp.float32).reshape(TOKENS, HEADS, HDIM).sum(axis=1)
    key_sums = jax.ops.segment_sum(key_heads, jnp.repeat(cluster_ids, BLK), num_segments=CLUSTERS)
    centroids = key_sums / jnp.sqrt(lax.optimization_barrier(jnp.mean(key_sums * key_sums, axis=1, keepdims=True)) + 1e-06)
    return (grads_q, grads_k, grads_v, centroids)
```

```python
import math

import jax
import jax.numpy as jnp
from jax import lax
from jax.sharding import PartitionSpec as P

HDIM = 128
CLUS_DEV = 4


def exchange(pieces):
    return lax.all_to_all(pieces, "ctx", split_axis=0, concat_axis=0, tiled=True)


def shards(queries, keys, values, out_grad, cluster_ids):
    blocks = cluster_ids.shape[0]
    rows_dev, width = queries.shape
    block_rows = rows_dev // blocks
    owners = lax.axis_size("ctx")
    me = lax.axis_index("ctx")
    all_ids = lax.all_gather(cluster_ids, "ctx", tiled=True)
    order = jnp.argsort(all_ids // CLUS_DEV, stable=True)
    place = jnp.argsort(order, stable=True)
    row_ids = lax.dynamic_slice_in_dim(all_ids[order], me * blocks, blocks)

    sent = jnp.stack(
        [a.reshape(blocks, block_rows, width) for a in (queries, keys, values, out_grad)], axis=2
    )
    held = exchange(sent.swapaxes(0, 1).reshape(owners, blocks, 4 * width))
    held = held.reshape(owners * blocks, 4 * width)[order]
    own = exchange(held.reshape(owners, blocks, 4 * width))
    own = own.swapaxes(0, 1).reshape(rows_dev, 4 * width)
    q_own, k_own, v_own, g_own = jnp.split(own, 4, axis=1)

    score_scale = 1.0 / math.sqrt(HDIM)
    row_cluster = jnp.repeat(row_ids, block_rows)
    position = jnp.arange(rows_dev)
    allowed = (row_cluster[:, None] == row_cluster[None, :]) & (
        position[None, :] <= position[:, None]
    )
    scores = jnp.einsum("qd,kd->qk", q_own, k_own, preferred_element_type=jnp.float32)
    scores = jnp.where(allowed, scores * score_scale, -jnp.inf)
    exponent = jnp.exp(scores - jnp.max(scores, axis=1, keepdims=True))
    probs = exponent / jnp.sum(exponent, axis=1, keepdims=True)
    probs_low = probs.astype(jnp.bfloat16)
    attn_out = jnp.dot(probs_low, v_own, preferred_element_type=jnp.float32)
    delta_row = jnp.sum(g_own.astype(jnp.float32) * attn_out, axis=1, keepdims=True)
    grad_v = jnp.einsum("qk,qd->kd", probs_low, g_own, preferred_element_type=jnp.float32)
    dprob = jnp.einsum("qd,kd->qk", g_own, v_own, preferred_element_type=jnp.float32)
    dscore = (probs * (dprob - delta_row)).astype(jnp.bfloat16)
    grad_q = jnp.dot(dscore, k_own, preferred_element_type=jnp.float32) * score_scale
    grad_k = jnp.einsum("qk,qd->kd", dscore, q_own, preferred_element_type=jnp.float32)
    grad_k = grad_k * score_scale

    back = jnp.stack(
        [g.astype(jnp.bfloat16).reshape(blocks, block_rows, width) for g in (grad_q, grad_k, grad_v)],
        axis=2,
    )
    back = exchange(back.swapaxes(0, 1).reshape(owners, blocks, 3 * width))
    back = back.reshape(owners * blocks, 3 * width)[place]
    back = exchange(back.reshape(owners, blocks, 3 * width))
    back = back.swapaxes(0, 1).reshape(rows_dev, 3 * width)

    member = ((row_cluster % CLUS_DEV)[None, :] == jnp.arange(CLUS_DEV)[:, None]).astype(
        jnp.bfloat16
    )
    partial_sums = jnp.dot(member, k_own, preferred_element_type=jnp.float32)
    whole_sums = lax.psum(partial_sums, "head")
    centroids = whole_sums / jnp.sqrt(
        jnp.mean(whole_sums * whole_sums, axis=1, keepdims=True) + 1e-06
    )
    return (*jnp.split(back, 3, axis=1), centroids)


def solution(mesh):
    placed = (P("ctx", "head"), P("ctx", "head"), P("ctx", "head"), P("ctx", "head"), P("ctx"))
    return jax.shard_map(
        shards,
        mesh=mesh,
        in_specs=placed,
        out_specs=(P("ctx", "head"), P("ctx", "head"), P("ctx", "head"), P("ctx", None)),
        check_vma=False,
    )
```

```python
import functools
import math

import jax
import jax.numpy as jnp
from jax import lax
from jax.experimental import pallas as pl
from jax.experimental.pallas import tpu as pltpu
from jax.sharding import PartitionSpec as P

HDIM = 128
CLUS_DEV = 4
BLOCKS = 8
TILE = 16
RING_Y = 4
MESH = pl.DeviceIdType.MESH
NT = (((1,), (1,)), ((), ()))
F32 = jnp.float32
BF16 = jnp.bfloat16

IDS, IN_A, IN_B, OWN_A, OWN_B, GV, GQK, BACK_V, BACK_QK, CEN = range(10)


def iota(shape, dim):
    return lax.broadcasted_iota(jnp.int32, shape, dim)


def onehot(mask):
    return jnp.where(mask, 1.0, 0.0).astype(BF16)


def piece_row(r, block_rows):
    return ((r >> 1) & (BLOCKS - 1)) * block_rows + 2 * (r >> 4) + (r & 1)


def lanes(column, width):
    return jnp.concatenate([column] * (width // HDIM), axis=1) if width > HDIM else column


def kernel(
    n_ctx, n_head,
    q_ref, k_ref, v_ref, g_ref, id_ref,
    dq_ref, dk_ref, dv_ref, cen_ref,
    pack, ids_all, idc, in1, in2, own, res, mid1, mid2, back,
    sort_mat, unsort_mat, probs, dscore, k_t, cen_buf, send_sem, recv_sem,
):
    me = lax.axis_index("ctx")
    head = lax.axis_index("head")
    core = head % 2
    my_z, my_y = me // RING_Y, me % RING_Y
    n_z = n_ctx // RING_Y
    pairs = n_ctx // 2
    rows = BLOCKS * n_ctx
    grows = TILE * n_ctx
    block_rows = n_ctx
    scale = 1.0 / math.sqrt(HDIM)

    def peer(i):
        m = 2 * (i // 8) + i % 2
        dz = n_z // 2 + (1 - 2 * (m % 2)) * ((m + 1) // 2)
        dy = (i // 2 + 1) % RING_Y
        return ((my_z + dz) % n_z) * RING_Y + (my_y + dy) % RING_Y

    def half_tile(p):
        return (p // RING_Y // 2) * RING_Y + p % RING_Y

    def in_half(p):
        return (p // RING_Y) % 2 == core

    def send(src, dst, phase, p):
        pltpu.make_async_remote_copy(
            src_ref=src, dst_ref=dst, send_sem=send_sem.at[phase], recv_sem=recv_sem.at[phase],
            device_id={"ctx": p}, device_id_type=MESH,
        ).start()

    def await_copy(ref, sem):
        pltpu.make_async_copy(ref, ref, sem).wait()

    barrier = pltpu.get_barrier_semaphore()

    @pl.loop(0, n_ctx - 1)
    def _(i):
        pl.semaphore_signal(barrier, 1, device_id={"ctx": peer(i)}, device_id_type=MESH)

    @pl.loop(1, n_head)
    def _(i):
        pl.semaphore_signal(
            barrier, 1, device_id={"head": (head + i) % n_head}, device_id_type=MESH
        )

    chunk = min(128, rows)
    every = jnp.concatenate([q_ref[...], k_ref[...], v_ref[...], g_ref[...]], axis=1)

    @pl.loop(0, rows // chunk)
    def _(c):
        source = piece_row(iota((chunk, rows), 0) + c * chunk, block_rows)
        picked = jnp.dot(
            onehot(source == iota((chunk, rows), 1)), every, preferred_element_type=F32
        ).astype(BF16)
        tiles = chunk // TILE
        for a in range(4):
            pack[pl.ds(a * pairs + c * tiles, tiles)] = picked[
                :, a * HDIM : (a + 1) * HDIM
            ].reshape(tiles, TILE, HDIM)

    ids_all[me] = id_ref[...]
    in1[0, me] = pack[me]
    in1[1, me] = pack[n_ctx + me]

    pl.semaphore_wait(barrier, n_ctx - 1 + n_head - 1)

    @pl.loop(0, n_ctx - 1)
    def _(i):
        p = peer(i)
        send(id_ref, ids_all.at[me], IDS, p)
        send(pack.at[p], in1.at[0, me], IN_A, p)

    @pl.loop(0, n_ctx - 1)
    def _(i):
        p = peer(i)
        send(pack.at[n_ctx + p], in1.at[1, me], IN_B, p)

    await_copy(ids_all.at[pl.ds(0, n_ctx - 1)], recv_sem.at[IDS])
    id_rows = ids_all[...].reshape(n_ctx, HDIM).astype(BF16)
    spread = jnp.dot(
        onehot((iota((grows, n_ctx), 0) >> 4) == iota((grows, n_ctx), 1)),
        id_rows, preferred_element_type=F32,
    )
    keep = ((iota((grows, HDIM), 0) >> 1) & (BLOCKS - 1)) == iota((grows, HDIM), 1)
    spread = jnp.where(keep, spread, 0.0).astype(BF16)
    idc[...] = jnp.dot(spread, jnp.ones((HDIM, HDIM), BF16), preferred_element_type=F32)
    id_lane = lax.dot_general(jnp.ones((8, HDIM), BF16), spread, NT, preferred_element_type=F32)
    owner_lane = jnp.floor(id_lane[0:1] * (1.0 / CLUS_DEV))

    step = min(128, grows)

    def rank(c, before):
        owner = jnp.floor(idc[pl.ds(c * step, step), :] * (1.0 / CLUS_DEV))
        same = lanes(owner, grows) == owner_lane
        row = (iota((step, grows), 0) + c * step) >> 1
        column = iota((step, grows), 1) >> 1
        before = before + jnp.sum(
            jnp.where(same & (row < column), 1.0, 0.0), axis=0, keepdims=True
        )
        ahead = jnp.dot(
            onehot(same & (column < row)), jnp.ones((grows, HDIM), BF16),
            preferred_element_type=F32,
        )
        parity = (iota((step, HDIM), 0) & 1).astype(F32)
        place = TILE * owner + ahead + parity
        unsort_mat[pl.ds(c * step, step), :] = onehot(
            lanes(place, grows) == iota((step, grows), 1).astype(F32)
        )
        return before

    before = lax.fori_loop(0, grows // step, rank, jnp.zeros((1, grows), F32))
    place_lane = TILE * owner_lane + before + (iota((1, grows), 1) & 1).astype(F32)

    @pl.loop(0, grows // step)
    def _(c):
        row = (iota((step, grows), 0) + c * step).astype(F32)
        sort_mat[pl.ds(c * step, step), :] = onehot(row == place_lane)

    id_tile = jnp.dot(
        sort_mat[pl.ds(pl.multiple_of(me * TILE, TILE), TILE), :], idc[...].astype(BF16),
        preferred_element_type=F32,
    )
    id_own = jnp.concatenate([id_tile] * pairs, axis=0)
    id_own_lane = lax.dot_general(
        onehot(iota((8, HDIM), 1) == 0), id_own.astype(BF16), NT, preferred_element_type=F32
    )

    wide = min(256, grows)

    def permute(mat, src, dst, which):
        data = src[which].reshape(grows, HDIM)

        @pl.loop(0, grows // wide)
        def _(c):
            moved = jnp.dot(
                mat[pl.ds(c * wide, wide), :], data, preferred_element_type=F32
            ).astype(BF16)
            dst[which, pl.ds(c * (wide // TILE), wide // TILE)] = moved.reshape(
                wide // TILE, TILE, HDIM
            )

    for which, (arrive, leave) in enumerate(((IN_A, OWN_A), (IN_B, OWN_B))):
        await_copy(in1.at[which, pl.ds(0, n_ctx - 1)], recv_sem.at[arrive])
        permute(sort_mat, in1, in2, which)
        own[which, me] = in2[which, me]

        @pl.loop(0, n_ctx - 1)
        def _(i):
            p = peer(i)
            send(in2.at[which, p], own.at[which, me], leave, p)

    await_copy(own.at[0, pl.ds(0, n_ctx - 1)], recv_sem.at[OWN_A])
    q_own = own[0, pl.ds(0, pairs)].reshape(rows, HDIM)
    k_own = own[0, pl.ds(pairs, pairs)].reshape(rows, HDIM)
    part = min(256, rows)

    for c in range(rows // part):
        cut = slice(c * part, (c + 1) * part)
        scores = (
            lax.dot_general(k_own, q_own[cut], NT, preferred_element_type=F32) * scale
        )
        key_pos = piece_row(iota((rows, part), 0), block_rows)
        query_pos = piece_row(iota((rows, part), 1) + c * part, block_rows)
        allowed = (lanes(id_own, part)[:, :part] == id_own_lane[0:1, cut]) & (key_pos <= query_pos)
        scores = jnp.where(allowed, scores, -jnp.inf)
        exponent = jnp.exp(scores - jnp.max(scores, axis=0, keepdims=True))
        probs[:, cut] = exponent * (1.0 / jnp.sum(exponent, axis=0, keepdims=True))

    local = (id_own_lane - (CLUS_DEV * me).astype(F32)) == iota((8, rows), 0).astype(F32)
    cen_buf[head] = jnp.dot(onehot(local), k_own, preferred_element_type=F32)

    @pl.loop(1, n_head)
    def _(i):
        pltpu.make_async_remote_copy(
            src_ref=cen_buf.at[head], dst_ref=cen_buf.at[head],
            send_sem=send_sem.at[CEN], recv_sem=recv_sem.at[CEN],
            device_id={"head": (head + i) % n_head}, device_id_type=MESH,
        ).start()

    k_t[...] = k_own.astype(F32).T.astype(BF16)

    await_copy(own.at[1, pl.ds(0, n_ctx - 1)], recv_sem.at[OWN_B])
    v_own = own[1, pl.ds(0, pairs)].reshape(rows, HDIM)
    g_own = own[1, pl.ds(pairs, pairs)].reshape(rows, HDIM)

    values_grad = jnp.dot(probs[...].astype(BF16), g_own, preferred_element_type=F32)
    res[pl.ds(2 * pairs, pairs)] = values_grad.astype(BF16).reshape(pairs, TILE, HDIM)

    @pl.when(in_half(me))
    def _():
        mid1[1, me] = res[2 * pairs + half_tile(me)]

    @pl.loop(0, n_ctx - 1)
    def _(i):
        p = peer(i)

        @pl.when(in_half(p))
        def _():
            send(res.at[2 * pairs + half_tile(p)], mid1.at[1, me], GV, p)

    for c in range(rows // part):
        cut = slice(c * part, (c + 1) * part)
        dprob = lax.dot_general(v_own, g_own[cut], NT, preferred_element_type=F32)
        prob = probs[:, cut]
        delta = jnp.sum(prob.astype(BF16).astype(F32) * dprob, axis=0, keepdims=True)
        dscore[:, cut] = (prob * (dprob - delta)).astype(BF16)

    keys_grad = jnp.dot(dscore[...], q_own, preferred_element_type=F32) * scale
    res[pl.ds(pairs, pairs)] = keys_grad.astype(BF16).reshape(pairs, TILE, HDIM)
    queries_grad = jnp.dot(k_t[...], dscore[...], preferred_element_type=F32) * scale
    res[pl.ds(0, pairs)] = queries_grad.T.astype(BF16).reshape(pairs, TILE, HDIM)
    mid1[0, me] = res[me]

    @pl.loop(0, n_ctx - 1)
    def _(i):
        p = peer(i)
        send(res.at[p], mid1.at[0, me], GQK, p)

    @pl.when(in_half(me))
    def _():
        await_copy(mid1.at[1, pl.ds(0, n_ctx - 1)], recv_sem.at[GV])
        permute(unsort_mat, mid1, mid2, 1)
        back[2 * pairs + half_tile(me)] = mid2[1, me]

        @pl.loop(0, n_ctx - 1)
        def _(i):
            p = peer(i)
            send(mid2.at[1, p], back.at[2 * pairs + half_tile(me)], BACK_V, p)

    await_copy(mid1.at[0, pl.ds(0, n_ctx - 1)], recv_sem.at[GQK])
    permute(unsort_mat, mid1, mid2, 0)
    back[me] = mid2[0, me]

    @pl.loop(0, n_ctx - 1)
    def _(i):
        p = peer(i)
        send(mid2.at[0, p], back.at[me], BACK_QK, p)

    await_copy(cen_buf.at[pl.ds(0, n_head - 1)], recv_sem.at[CEN])
    whole = cen_buf[0]
    for h in range(1, n_head):
        whole = whole + cen_buf[h]
    centroids = whole / jnp.sqrt(jnp.mean(whole * whole, axis=1, keepdims=True) + 1e-06)
    cen_ref[...] = centroids[:CLUS_DEV]

    def unpack(first, out):
        data = back[pl.ds(first, pairs)].reshape(rows, HDIM)

        @pl.loop(0, rows // chunk)
        def _(c):
            source = piece_row(iota((chunk, rows), 1), block_rows)
            picked = jnp.dot(
                onehot(source == iota((chunk, rows), 0) + c * chunk), data,
                preferred_element_type=F32,
            )
            out[pl.ds(c * chunk, chunk), :] = picked.astype(BF16)

    @pl.when(in_half(me))
    def _():
        await_copy(back.at[pl.ds(2 * pairs, pairs - 1)], recv_sem.at[BACK_V])
        await_copy(res.at[pl.ds(2 * pairs, pairs - 1)], send_sem.at[GV])
        await_copy(mid2.at[1, pl.ds(0, n_ctx - 1)], send_sem.at[BACK_V])

    @pl.when(jnp.logical_not(in_half(me)))
    def _():
        await_copy(back.at[pl.ds(2 * pairs, pairs)], recv_sem.at[BACK_V])
        await_copy(res.at[pl.ds(2 * pairs, pairs)], send_sem.at[GV])

    unpack(2 * pairs, dv_ref)
    await_copy(back.at[pl.ds(0, n_ctx - 1)], recv_sem.at[BACK_QK])
    unpack(0, dq_ref)
    unpack(pairs, dk_ref)

    await_copy(ids_all.at[pl.ds(0, n_ctx - 1)], send_sem.at[IDS])
    await_copy(pack.at[pl.ds(0, n_ctx - 1)], send_sem.at[IN_A])
    await_copy(pack.at[pl.ds(0, n_ctx - 1)], send_sem.at[IN_B])
    await_copy(in2.at[0, pl.ds(0, n_ctx - 1)], send_sem.at[OWN_A])
    await_copy(in2.at[1, pl.ds(0, n_ctx - 1)], send_sem.at[OWN_B])
    await_copy(res.at[pl.ds(0, n_ctx - 1)], send_sem.at[GQK])
    await_copy(mid2.at[0, pl.ds(0, n_ctx - 1)], send_sem.at[BACK_QK])
    await_copy(cen_buf.at[pl.ds(0, n_head - 1)], send_sem.at[CEN])


def shards(queries, keys, values, out_grad, cluster_ids):
    n_ctx, n_head = lax.axis_size("ctx"), lax.axis_size("head")
    rows = queries.shape[0]
    pairs, grows = n_ctx // 2, TILE * n_ctx
    id_row = jnp.pad(cluster_ids.astype(F32), (0, HDIM - BLOCKS)).reshape(1, HDIM)
    vmem = pl.BlockSpec(memory_space=pltpu.VMEM)
    grad = jax.ShapeDtypeStruct((rows, HDIM), BF16)
    return pl.pallas_call(
        functools.partial(kernel, n_ctx, n_head),
        out_shape=(grad, grad, grad, jax.ShapeDtypeStruct((CLUS_DEV, HDIM), F32)),
        in_specs=[vmem] * 5,
        out_specs=(vmem,) * 4,
        scratch_shapes=[
            pltpu.VMEM((4 * pairs, TILE, HDIM), BF16),
            pltpu.VMEM((n_ctx, 1, HDIM), F32),
            pltpu.VMEM((grows, HDIM), F32),
            pltpu.VMEM((2, n_ctx, TILE, HDIM), BF16),
            pltpu.VMEM((2, n_ctx, TILE, HDIM), BF16),
            pltpu.VMEM((2, n_ctx, TILE, HDIM), BF16),
            pltpu.VMEM((3 * pairs, TILE, HDIM), BF16),
            pltpu.VMEM((2, n_ctx, TILE, HDIM), BF16),
            pltpu.VMEM((2, n_ctx, TILE, HDIM), BF16),
            pltpu.VMEM((3 * pairs, TILE, HDIM), BF16),
            pltpu.VMEM((grows, grows), BF16),
            pltpu.VMEM((grows, grows), BF16),
            pltpu.VMEM((rows, rows), F32),
            pltpu.VMEM((rows, rows), BF16),
            pltpu.VMEM((HDIM, rows), BF16),
            pltpu.VMEM((n_head, 8, HDIM), F32),
            pltpu.SemaphoreType.DMA((10,)),
            pltpu.SemaphoreType.DMA((10,)),
        ],
        compiler_params=pltpu.CompilerParams(
            collective_id=0, has_side_effects=True, vmem_limit_bytes=48 * 2**20
        ),
        name="routing_attention",
    )(queries, keys, values, out_grad, id_row)


def solution(mesh):
    placed = (P("ctx", "head"), P("ctx", "head"), P("ctx", "head"), P("ctx", "head"), P("ctx"))
    return jax.shard_map(
        shards,
        mesh=mesh,
        in_specs=placed,
        out_specs=(P("ctx", "head"), P("ctx", "head"), P("ctx", "head"), P("ctx", None)),
        check_vma=False,
    )
```

```python
import functools
import math

import jax
import jax.numpy as jnp
from jax import lax
from jax.experimental import pallas as pl
from jax.experimental.pallas import tpu as pltpu
from jax.sharding import PartitionSpec as P

HDIM = 128
CLUS_DEV = 4
BLOCKS = 8
TILE = 16
RING_Y = 4
MESH = pl.DeviceIdType.MESH
NT = (((1,), (1,)), ((), ()))
F32 = jnp.float32
BF16 = jnp.bfloat16

IDS, IN_A, IN_B, OWN_A, OWN_V, OWN_G, GV, GQK, BACK_V, BACK_QK, CEN = range(11)


def iota(shape, dim):
    return lax.broadcasted_iota(jnp.int32, shape, dim)


def onehot(mask):
    return jnp.where(mask, 1.0, 0.0).astype(BF16)


def piece_row(r, block_rows):
    return ((r >> 1) & (BLOCKS - 1)) * block_rows + 2 * (r >> 4) + (r & 1)


def lanes(column, width):
    return jnp.concatenate([column] * (width // HDIM), axis=1) if width > HDIM else column


def unpack(tiles, out):
    rows = tiles.shape[0] * TILE
    data = tiles.reshape(rows, HDIM)
    chunk = min(256, rows)
    for c in range(rows // chunk):
        source = piece_row(iota((chunk, rows), 1), rows // BLOCKS)
        picked = jnp.dot(
            onehot(source == iota((chunk, rows), 0) + c * chunk), data,
            preferred_element_type=F32,
        )
        out[pl.ds(c * chunk, chunk), :] = picked.astype(BF16)


def kernel(
    n_ctx, n_head,
    q_ref, k_ref, v_ref, g_ref, id_ref,
    back, dv_ref, cen_ref,
    staged, id_words, id_row, pack, ids_all, idc, in1, in2, own, res, mid1, mid2, back_v,
    sort_mat, unsort_mat, probs, probs_low, dscore, k_t, cen_buf, load_sem, send_sem, recv_sem,
):
    me = lax.axis_index("ctx")
    head = lax.axis_index("head")
    core = head % 2
    my_z, my_y = me // RING_Y, me % RING_Y
    n_z = n_ctx // RING_Y
    pairs = n_ctx // 2
    rows = BLOCKS * n_ctx
    grows = TILE * n_ctx
    block_rows = n_ctx
    scale = 1.0 / math.sqrt(HDIM)

    def peer(i):
        m = 2 * (i // 8) + i % 2
        dz = n_z // 2 + (1 - 2 * (m % 2)) * ((m + 1) // 2)
        dy = (i // 2 + 1) % RING_Y
        return ((my_z + dz) % n_z) * RING_Y + (my_y + dy) % RING_Y

    def half_tile(p):
        return (p // RING_Y // 2) * RING_Y + p % RING_Y

    def half(p):
        return (p // RING_Y + core + 1) % 2

    def send(src, dst, phase, p):
        pltpu.make_async_remote_copy(
            src_ref=src, dst_ref=dst, send_sem=send_sem.at[phase], recv_sem=recv_sem.at[phase],
            device_id={"ctx": p}, device_id_type=MESH,
        ).start()

    def await_copy(ref, sem):
        pltpu.make_async_copy(ref, ref, sem).wait()

    barrier = pltpu.get_barrier_semaphore()

    @pl.loop(0, n_ctx - 1)
    def _(i):
        pl.semaphore_signal(barrier, 1, device_id={"ctx": peer(i)}, device_id_type=MESH)

    @pl.loop(1, n_head)
    def _(i):
        pl.semaphore_signal(
            barrier, 1, device_id={"head": (head + i) % n_head}, device_id_type=MESH
        )

    loads = [
        pltpu.make_async_copy(ref, staged.at[a], load_sem.at[a])
        for a, ref in enumerate((q_ref, k_ref, v_ref, g_ref))
    ] + [pltpu.make_async_copy(id_ref, id_words, load_sem.at[4])]
    for load in loads:
        load.start()
    for load in loads:
        load.wait()

    chunk = min(128, rows)
    every = jnp.concatenate([staged[a] for a in range(4)], axis=1)

    @pl.loop(0, rows // chunk)
    def _(c):
        source = piece_row(iota((chunk, rows), 0) + c * chunk, block_rows)
        picked = jnp.dot(
            onehot(source == iota((chunk, rows), 1)), every, preferred_element_type=F32
        ).astype(BF16)
        tiles = chunk // TILE
        for a in range(4):
            pack[pl.ds(a * pairs + c * tiles, tiles)] = picked[
                :, a * HDIM : (a + 1) * HDIM
            ].reshape(tiles, TILE, HDIM)

    words = jnp.zeros((1, HDIM), jnp.int32)
    for b in range(BLOCKS):
        words = jnp.where(iota((1, HDIM), 1) == b, id_words[b], words)
    id_row[...] = words.astype(F32)
    ids_all[me] = id_row[...]

    def second(p):
        return n_ctx + half(p) * pairs + half_tile(p)

    in1[0, me] = pack[me]
    in1[1, me] = pack[second(me)]

    pl.semaphore_wait(barrier, n_ctx - 1 + n_head - 1)

    @pl.loop(0, n_ctx - 1)
    def _(i):
        p = peer(i)
        send(id_row, ids_all.at[me], IDS, p)
        send(pack.at[p], in1.at[0, me], IN_A, p)

    @pl.loop(0, n_ctx - 1)
    def _(i):
        p = peer(i)
        send(pack.at[second(p)], in1.at[1, me], IN_B, p)

    await_copy(ids_all.at[pl.ds(0, n_ctx - 1)], recv_sem.at[IDS])
    id_rows = ids_all[...].reshape(n_ctx, HDIM).astype(BF16)
    spread = jnp.dot(
        onehot((iota((grows, n_ctx), 0) >> 4) == iota((grows, n_ctx), 1)),
        id_rows, preferred_element_type=F32,
    )
    keep = ((iota((grows, HDIM), 0) >> 1) & (BLOCKS - 1)) == iota((grows, HDIM), 1)
    spread = jnp.where(keep, spread, 0.0).astype(BF16)
    idc[...] = jnp.dot(spread, jnp.ones((HDIM, HDIM), BF16), preferred_element_type=F32)
    id_lane = lax.dot_general(jnp.ones((8, HDIM), BF16), spread, NT, preferred_element_type=F32)
    owner_lane = jnp.floor(id_lane[0:1] * (1.0 / CLUS_DEV))

    step = min(128, grows)

    def rank(c, before):
        owner = jnp.floor(idc[pl.ds(c * step, step), :] * (1.0 / CLUS_DEV))
        same = lanes(owner, grows) == owner_lane
        row = (iota((step, grows), 0) + c * step) >> 1
        column = iota((step, grows), 1) >> 1
        before = before + jnp.sum(
            jnp.where(same & (row < column), 1.0, 0.0), axis=0, keepdims=True
        )
        ahead = jnp.dot(
            onehot(same & (column < row)), jnp.ones((grows, HDIM), BF16),
            preferred_element_type=F32,
        )
        parity = (iota((step, HDIM), 0) & 1).astype(F32)
        place = TILE * owner + ahead + parity
        unsort_mat[pl.ds(c * step, step), :] = onehot(
            lanes(place, grows) == iota((step, grows), 1).astype(F32)
        )
        return before

    before = lax.fori_loop(0, grows // step, rank, jnp.zeros((1, grows), F32))
    place_lane = TILE * owner_lane + before + (iota((1, grows), 1) & 1).astype(F32)

    @pl.loop(0, grows // step)
    def _(c):
        row = (iota((step, grows), 0) + c * step).astype(F32)
        sort_mat[pl.ds(c * step, step), :] = onehot(row == place_lane)

    id_tile = jnp.dot(
        sort_mat[pl.ds(pl.multiple_of(me * TILE, TILE), TILE), :], idc[...].astype(BF16),
        preferred_element_type=F32,
    )
    id_own = jnp.concatenate([id_tile] * pairs, axis=0)
    id_own_lane = lax.dot_general(
        onehot(iota((8, HDIM), 1) == 0), id_own.astype(BF16), NT, preferred_element_type=F32
    )

    wide = min(256, grows)

    def permute(mat, src, dst, which):
        data = src[which].reshape(grows, HDIM)

        @pl.loop(0, grows // wide)
        def _(c):
            moved = jnp.dot(
                mat[pl.ds(c * wide, wide), :], data, preferred_element_type=F32
            ).astype(BF16)
            dst[which, pl.ds(c * (wide // TILE), wide // TILE)] = moved.reshape(
                wide // TILE, TILE, HDIM
            )

    def hand_out(which, slot, phase):
        own[which, slot] = in2[which, me]

        @pl.loop(0, n_ctx - 1)
        def _(i):
            p = peer(i)
            send(in2.at[which, p], own.at[which, slot], phase, p)

    await_copy(in1.at[0, pl.ds(0, n_ctx - 1)], recv_sem.at[IN_A])
    permute(sort_mat, in1, in2, 0)
    hand_out(0, me, OWN_A)
    await_copy(in1.at[1, pl.ds(0, n_ctx - 1)], recv_sem.at[IN_B])
    permute(sort_mat, in1, in2, 1)

    @pl.when(half(me) == 1)
    def _():
        hand_out(1, pairs + half_tile(me), OWN_G)

    await_copy(own.at[0, pl.ds(0, n_ctx - 1)], recv_sem.at[OWN_A])
    q_own = own[0, pl.ds(0, pairs)].reshape(rows, HDIM)
    k_own = own[0, pl.ds(pairs, pairs)].reshape(rows, HDIM)
    part = min(256, rows)

    for c in range(rows // part):
        cut = slice(c * part, (c + 1) * part)
        scores = (
            lax.dot_general(k_own, q_own[cut], NT, preferred_element_type=F32) * scale
        )
        key_pos = piece_row(iota((rows, part), 0), block_rows)
        query_pos = piece_row(iota((rows, part), 1) + c * part, block_rows)
        allowed = (lanes(id_own, part)[:, :part] == id_own_lane[0:1, cut]) & (key_pos <= query_pos)
        scores = jnp.where(allowed, scores, -jnp.inf)
        exponent = jnp.exp(scores - jnp.max(scores, axis=0, keepdims=True))
        probs[:, cut] = exponent * (1.0 / jnp.sum(exponent, axis=0, keepdims=True))

    @pl.when(half(me) == 0)
    def _():
        hand_out(1, half_tile(me), OWN_V)

    local = (id_own_lane - (CLUS_DEV * me).astype(F32)) == iota((8, rows), 0).astype(F32)
    cen_buf[head] = jnp.dot(onehot(local), k_own, preferred_element_type=F32)

    @pl.loop(1, n_head)
    def _(i):
        pltpu.make_async_remote_copy(
            src_ref=cen_buf.at[head], dst_ref=cen_buf.at[head],
            send_sem=send_sem.at[CEN], recv_sem=recv_sem.at[CEN],
            device_id={"head": (head + i) % n_head}, device_id_type=MESH,
        ).start()

    k_t[...] = k_own.astype(F32).T.astype(BF16)

    def await_half(first, remote, sem):
        @pl.when(half(me) == remote)
        def _():
            await_copy(own.at[1, pl.ds(first, pairs)], sem)

        @pl.when(half(me) == 1 - remote)
        def _():
            await_copy(own.at[1, pl.ds(first, pairs - 1)], sem)

    probs_low[...] = probs[...].astype(BF16)
    await_half(pairs, 0, recv_sem.at[OWN_G])
    g_own = own[1, pl.ds(pairs, pairs)].reshape(rows, HDIM)

    values_grad = jnp.dot(probs_low[...], g_own, preferred_element_type=F32)
    res[pl.ds(2 * pairs, pairs)] = values_grad.astype(BF16).reshape(pairs, TILE, HDIM)

    @pl.when(half(me) == 1)
    def _():
        mid1[1, me] = res[2 * pairs + half_tile(me)]

    @pl.loop(0, n_ctx - 1)
    def _(i):
        p = peer(i)

        @pl.when(half(p) == 1)
        def _():
            send(res.at[2 * pairs + half_tile(p)], mid1.at[1, me], GV, p)

    await_half(0, 1, recv_sem.at[OWN_V])
    v_own = own[1, pl.ds(0, pairs)].reshape(rows, HDIM)

    for c in range(rows // part):
        cut = slice(c * part, (c + 1) * part)
        dprob = lax.dot_general(v_own, g_own[cut], NT, preferred_element_type=F32)
        prob = probs[:, cut]
        delta = jnp.sum(probs_low[:, cut].astype(F32) * dprob, axis=0, keepdims=True)
        dscore[:, cut] = (prob * (dprob - delta)).astype(BF16)

    keys_grad = jnp.dot(dscore[...], q_own, preferred_element_type=F32) * scale
    res[pl.ds(pairs, pairs)] = keys_grad.astype(BF16).reshape(pairs, TILE, HDIM)
    queries_grad = jnp.dot(k_t[...], dscore[...], preferred_element_type=F32) * scale
    res[pl.ds(0, pairs)] = queries_grad.T.astype(BF16).reshape(pairs, TILE, HDIM)
    mid1[0, me] = res[me]

    @pl.loop(0, n_ctx - 1)
    def _(i):
        p = peer(i)
        send(res.at[p], mid1.at[0, me], GQK, p)

    @pl.when(half(me) == 1)
    def _():
        await_copy(mid1.at[1, pl.ds(0, n_ctx - 1)], recv_sem.at[GV])
        permute(unsort_mat, mid1, mid2, 1)
        back_v[half_tile(me)] = mid2[1, me]

        @pl.loop(0, n_ctx - 1)
        def _(i):
            p = peer(i)
            send(mid2.at[1, p], back_v.at[half_tile(me)], BACK_V, p)

    await_copy(mid1.at[0, pl.ds(0, n_ctx - 1)], recv_sem.at[GQK])
    permute(unsort_mat, mid1, mid2, 0)
    back[me] = mid2[0, me]

    @pl.loop(0, n_ctx - 1)
    def _(i):
        p = peer(i)
        send(mid2.at[0, p], back.at[me], BACK_QK, p)

    await_copy(cen_buf.at[pl.ds(0, n_head - 1)], recv_sem.at[CEN])
    whole = cen_buf[0]
    for h in range(1, n_head):
        whole = whole + cen_buf[h]
    centroids = whole / jnp.sqrt(jnp.mean(whole * whole, axis=1, keepdims=True) + 1e-06)
    cen_ref[...] = centroids[:CLUS_DEV]

    @pl.when(half(me) == 1)
    def _():
        await_copy(back_v.at[pl.ds(0, pairs - 1)], recv_sem.at[BACK_V])
        await_copy(res.at[pl.ds(2 * pairs, pairs - 1)], send_sem.at[GV])
        await_copy(mid2.at[1, pl.ds(0, n_ctx - 1)], send_sem.at[BACK_V])

    @pl.when(half(me) == 0)
    def _():
        await_copy(back_v.at[pl.ds(0, pairs)], recv_sem.at[BACK_V])
        await_copy(res.at[pl.ds(2 * pairs, pairs)], send_sem.at[GV])

    unpack(back_v[...], dv_ref)
    await_copy(ids_all.at[pl.ds(0, n_ctx - 1)], send_sem.at[IDS])
    await_copy(pack.at[pl.ds(0, n_ctx - 1)], send_sem.at[IN_A])
    await_copy(pack.at[pl.ds(0, n_ctx - 1)], send_sem.at[IN_B])
    await_copy(in2.at[0, pl.ds(0, n_ctx - 1)], send_sem.at[OWN_A])
    await_copy(in2.at[1, pl.ds(0, n_ctx - 1)], send_sem.at[OWN_V + half(me)])
    await_copy(res.at[pl.ds(0, n_ctx - 1)], send_sem.at[GQK])
    await_copy(mid2.at[0, pl.ds(0, n_ctx - 1)], send_sem.at[BACK_QK])
    await_copy(cen_buf.at[pl.ds(0, n_head - 1)], send_sem.at[CEN])
    await_copy(back.at[pl.ds(0, n_ctx - 1)], recv_sem.at[BACK_QK])


def finish(back, dv_in, cen_in, dq_out, dk_out, dv_out, cen_out, grads, sem):
    pairs = back.shape[0] // 2
    stores = [
        pltpu.make_async_copy(dv_in, dv_out, sem.at[0]),
        pltpu.make_async_copy(cen_in, cen_out, sem.at[1]),
        pltpu.make_async_copy(grads.at[0], dq_out, sem.at[2]),
        pltpu.make_async_copy(grads.at[1], dk_out, sem.at[3]),
    ]
    stores[0].start()
    stores[1].start()
    for a in range(2):
        unpack(back[pl.ds(a * pairs, pairs)], grads.at[a])
        stores[2 + a].start()
    for store in stores:
        store.wait()


def shards(queries, keys, values, out_grad, cluster_ids):
    n_ctx, n_head = lax.axis_size("ctx"), lax.axis_size("head")
    rows = queries.shape[0]
    pairs, grows = n_ctx // 2, TILE * n_ctx
    vmem = pl.BlockSpec(memory_space=pltpu.VMEM)
    hbm = pl.BlockSpec(memory_space=pltpu.HBM)
    grad = jax.ShapeDtypeStruct((rows, HDIM), BF16)
    centroid = jax.ShapeDtypeStruct((CLUS_DEV, HDIM), F32)
    back, dv, cen = pl.pallas_call(
        functools.partial(kernel, n_ctx, n_head),
        out_shape=(jax.ShapeDtypeStruct((n_ctx, TILE, HDIM), BF16), grad, centroid),
        in_specs=[hbm] * 5,
        out_specs=(vmem,) * 3,
        scratch_shapes=[
            pltpu.VMEM((4, rows, HDIM), BF16),
            pltpu.SMEM((BLOCKS,), jnp.int32),
            pltpu.VMEM((1, HDIM), F32),
            pltpu.VMEM((4 * pairs, TILE, HDIM), BF16),
            pltpu.VMEM((n_ctx, 1, HDIM), F32),
            pltpu.VMEM((grows, HDIM), F32),
            pltpu.VMEM((2, n_ctx, TILE, HDIM), BF16),
            pltpu.VMEM((2, n_ctx, TILE, HDIM), BF16),
            pltpu.VMEM((2, n_ctx, TILE, HDIM), BF16),
            pltpu.VMEM((3 * pairs, TILE, HDIM), BF16),
            pltpu.VMEM((2, n_ctx, TILE, HDIM), BF16),
            pltpu.VMEM((2, n_ctx, TILE, HDIM), BF16),
            pltpu.VMEM((pairs, TILE, HDIM), BF16),
            pltpu.VMEM((grows, grows), BF16),
            pltpu.VMEM((grows, grows), BF16),
            pltpu.VMEM((rows, rows), F32),
            pltpu.VMEM((rows, rows), BF16),
            pltpu.VMEM((rows, rows), BF16),
            pltpu.VMEM((HDIM, rows), BF16),
            pltpu.VMEM((n_head, 8, HDIM), F32),
            pltpu.SemaphoreType.DMA((5,)),
            pltpu.SemaphoreType.DMA((11,)),
            pltpu.SemaphoreType.DMA((11,)),
        ],
        compiler_params=pltpu.CompilerParams(
            collective_id=0, has_side_effects=True
        ),
        name="routing_attention",
    )(queries, keys, values, out_grad, cluster_ids)
    return pl.pallas_call(
        finish,
        out_shape=(grad, grad, grad, centroid),
        in_specs=[vmem] * 3,
        out_specs=(hbm,) * 4,
        scratch_shapes=[
            pltpu.VMEM((2, rows, HDIM), BF16),
            pltpu.SemaphoreType.DMA((4,)),
        ],
        name="finish",
    )(back, dv, cen)


def solution(mesh):
    placed = (P("ctx", "head"), P("ctx", "head"), P("ctx", "head"), P("ctx", "head"), P("ctx"))
    return jax.shard_map(
        shards,
        mesh=mesh,
        in_specs=placed,
        out_specs=(P("ctx", "head"), P("ctx", "head"), P("ctx", "head"), P("ctx", None)),
        check_vma=False,
    )
```

```python
import functools
import math

import jax
import jax.numpy as jnp
from jax import lax
from jax.experimental import pallas as pl
from jax.experimental.pallas import tpu as pltpu
from jax.sharding import PartitionSpec as P

HDIM = 128
CLUS_DEV = 4
BLOCKS = 8
TILE = 16
RING_Y = 4
MESH = pl.DeviceIdType.MESH
NT = (((1,), (1,)), ((), ()))
F32 = jnp.float32
BF16 = jnp.bfloat16

IDS, IN_A, IN_B, OWN_A, OWN_V, OWN_G, GV, GQK, BACK_V, BACK_QK, CEN, SHARE = range(12)


def iota(shape, dim):
    return lax.broadcasted_iota(jnp.int32, shape, dim)


def onehot(mask):
    return jnp.where(mask, 1.0, 0.0).astype(BF16)


def piece_row(r, block_rows):
    return ((r >> 1) & (BLOCKS - 1)) * block_rows + 2 * (r >> 4) + (r & 1)


def lanes(column, width):
    return jnp.concatenate([column] * (width // HDIM), axis=1) if width > HDIM else column


def unpack(tiles, outs):
    rows = tiles[0].shape[0] * TILE
    data = jnp.concatenate([t.reshape(rows, HDIM) for t in tiles], axis=1)
    chunk = min(256, rows)
    for c in range(rows // chunk):
        source = piece_row(iota((chunk, rows), 1), rows // BLOCKS)
        picked = jnp.dot(
            onehot(source == iota((chunk, rows), 0) + c * chunk), data,
            preferred_element_type=F32,
        ).astype(BF16)
        for a, out in enumerate(outs):
            out[pl.ds(c * chunk, chunk), :] = picked[:, a * HDIM : (a + 1) * HDIM]


def kernel(
    n_ctx, n_head,
    q_ref, k_ref, v_ref, g_ref, id_ref,
    back, dv_ref, cen_ref,
    staged, id_words, id_row, pack, ids_all, idc, in1, in2, own, res, mid1, mid2, back_v,
    sort_mat, unsort_mat, probs, probs_low, dscore, k_t, cen_buf, cen_own, dv_own, load_sem, send_sem, recv_sem,
):
    me = lax.axis_index("ctx")
    head = lax.axis_index("head")
    core = head % 2
    my_z, my_y = me // RING_Y, me % RING_Y
    n_z = n_ctx // RING_Y
    pairs = n_ctx // 2
    rows = BLOCKS * n_ctx
    grows = TILE * n_ctx
    block_rows = n_ctx
    scale = 1.0 / math.sqrt(HDIM)

    def peer(i):
        m = 2 * (i // 8) + i % 2
        dz = n_z // 2 + (1 - 2 * (m % 2)) * ((m + 1) // 2)
        dy = (i // 2 + 1) % RING_Y
        return ((my_z + dz) % n_z) * RING_Y + (my_y + dy) % RING_Y

    def half_tile(p):
        return (p // RING_Y // 2) * RING_Y + p % RING_Y

    def half(p):
        return (p // RING_Y + core + 1) % 2

    def send(src, dst, phase, p):
        pltpu.make_async_remote_copy(
            src_ref=src, dst_ref=dst, send_sem=send_sem.at[phase], recv_sem=recv_sem.at[phase],
            device_id={"ctx": p}, device_id_type=MESH,
        ).start()

    def send_head(src, dst, phase, h):
        pltpu.make_async_remote_copy(
            src_ref=src, dst_ref=dst, send_sem=send_sem.at[phase], recv_sem=recv_sem.at[phase],
            device_id={"head": h}, device_id_type=MESH,
        ).start()

    def await_copy(ref, sem):
        pltpu.make_async_copy(ref, ref, sem).wait()

    barrier = pltpu.get_barrier_semaphore()

    @pl.loop(0, n_ctx - 1)
    def _(i):
        pl.semaphore_signal(barrier, 1, device_id={"ctx": peer(i)}, device_id_type=MESH)

    @pl.loop(1, n_head)
    def _(i):
        pl.semaphore_signal(
            barrier, 1, device_id={"head": (head + i) % n_head}, device_id_type=MESH
        )

    loads = [
        pltpu.make_async_copy(ref, staged.at[a], load_sem.at[a])
        for a, ref in enumerate((q_ref, k_ref, v_ref, g_ref))
    ] + [pltpu.make_async_copy(id_ref, id_words, load_sem.at[4])]
    for load in loads:
        load.start()
    for load in loads:
        load.wait()

    chunk = min(128, rows)
    every = jnp.concatenate([staged[a] for a in range(4)], axis=1)

    @pl.loop(0, rows // chunk)
    def _(c):
        source = piece_row(iota((chunk, rows), 0) + c * chunk, block_rows)
        picked = jnp.dot(
            onehot(source == iota((chunk, rows), 1)), every, preferred_element_type=F32
        ).astype(BF16)
        tiles = chunk // TILE
        for a in range(4):
            pack[pl.ds(a * pairs + c * tiles, tiles)] = picked[
                :, a * HDIM : (a + 1) * HDIM
            ].reshape(tiles, TILE, HDIM)

    words = jnp.zeros((1, HDIM), jnp.int32)
    for b in range(BLOCKS):
        words = jnp.where(iota((1, HDIM), 1) == b, id_words[b], words)
    id_row[...] = words.astype(F32)
    collects = me % n_head == head

    @pl.when(collects)
    def _():
        ids_all[me] = id_row[...]


    def second(p):
        return n_ctx + half(p) * pairs + half_tile(p)

    in1[0, me] = pack[me]
    in1[1, me] = pack[second(me)]

    pl.semaphore_wait(barrier, n_ctx - 1 + n_head - 1)

    @pl.loop(0, n_ctx - 1)
    def _(i):
        p = peer(i)

        @pl.when(p % n_head == head)
        def _():
            send(id_row, ids_all.at[me], IDS, p)

    @pl.loop(0, n_ctx - 1)
    def _(i):
        p = peer(i)
        send(pack.at[p], in1.at[0, me], IN_A, p)

    @pl.loop(0, n_ctx - 1)
    def _(i):
        p = peer(i)
        send(pack.at[second(p)], in1.at[1, me], IN_B, p)

    @pl.when(collects)
    def _():
        await_copy(ids_all.at[pl.ds(0, n_ctx - 1)], recv_sem.at[IDS])

        @pl.loop(1, n_head)
        def _(i):
            send_head(ids_all, ids_all, SHARE, (head + i) % n_head)

    @pl.when(jnp.logical_not(collects))
    def _():
        await_copy(ids_all, recv_sem.at[SHARE])

    id_rows = ids_all[...].reshape(n_ctx, HDIM).astype(BF16)
    spread = jnp.dot(
        onehot((iota((grows, n_ctx), 0) >> 4) == iota((grows, n_ctx), 1)),
        id_rows, preferred_element_type=F32,
    )
    keep = ((iota((grows, HDIM), 0) >> 1) & (BLOCKS - 1)) == iota((grows, HDIM), 1)
    spread = jnp.where(keep, spread, 0.0).astype(BF16)
    idc[...] = jnp.dot(spread, jnp.ones((HDIM, HDIM), BF16), preferred_element_type=F32)
    id_lane = lax.dot_general(jnp.ones((8, HDIM), BF16), spread, NT, preferred_element_type=F32)
    owner_lane = jnp.floor(id_lane[0:1] * (1.0 / CLUS_DEV))

    step = min(128, grows)

    def rank(c, before):
        owner = jnp.floor(idc[pl.ds(c * step, step), :] * (1.0 / CLUS_DEV))
        same = lanes(owner, grows) == owner_lane
        row = (iota((step, grows), 0) + c * step) >> 1
        column = iota((step, grows), 1) >> 1
        before = before + jnp.sum(
            jnp.where(same & (row < column), 1.0, 0.0), axis=0, keepdims=True
        )
        ahead = jnp.dot(
            onehot(same & (column < row)), jnp.ones((grows, HDIM), BF16),
            preferred_element_type=F32,
        )
        parity = (iota((step, HDIM), 0) & 1).astype(F32)
        place = TILE * owner + ahead + parity
        unsort_mat[pl.ds(c * step, step), :] = onehot(
            lanes(place, grows) == iota((step, grows), 1).astype(F32)
        )
        return before

    before = lax.fori_loop(0, grows // step, rank, jnp.zeros((1, grows), F32))
    place_lane = TILE * owner_lane + before + (iota((1, grows), 1) & 1).astype(F32)

    @pl.loop(0, grows // step)
    def _(c):
        row = (iota((step, grows), 0) + c * step).astype(F32)
        sort_mat[pl.ds(c * step, step), :] = onehot(row == place_lane)

    id_tile = jnp.dot(
        sort_mat[pl.ds(pl.multiple_of(me * TILE, TILE), TILE), :], idc[...].astype(BF16),
        preferred_element_type=F32,
    )
    id_own = jnp.concatenate([id_tile] * pairs, axis=0)
    id_own_lane = lax.dot_general(
        onehot(iota((8, HDIM), 1) == 0), id_own.astype(BF16), NT, preferred_element_type=F32
    )

    wide = min(256, grows)

    def permute(mat, src, dst, which):
        data = src[which].reshape(grows, HDIM)

        @pl.loop(0, grows // wide)
        def _(c):
            moved = jnp.dot(
                mat[pl.ds(c * wide, wide), :], data, preferred_element_type=F32
            ).astype(BF16)
            dst[which, pl.ds(c * (wide // TILE), wide // TILE)] = moved.reshape(
                wide // TILE, TILE, HDIM
            )

    def hand_out(which, slot, phase):
        own[which, slot] = in2[which, me]

        @pl.loop(0, n_ctx - 1)
        def _(i):
            p = peer(i)
            send(in2.at[which, p], own.at[which, slot], phase, p)

    await_copy(in1.at[0, pl.ds(0, n_ctx - 1)], recv_sem.at[IN_A])
    permute(sort_mat, in1, in2, 0)
    hand_out(0, me, OWN_A)
    await_copy(in1.at[1, pl.ds(0, n_ctx - 1)], recv_sem.at[IN_B])
    permute(sort_mat, in1, in2, 1)

    @pl.when(half(me) == 1)
    def _():
        hand_out(1, pairs + half_tile(me), OWN_G)

    await_copy(own.at[0, pl.ds(0, n_ctx - 1)], recv_sem.at[OWN_A])
    q_own = own[0, pl.ds(0, pairs)].reshape(rows, HDIM)
    k_own = own[0, pl.ds(pairs, pairs)].reshape(rows, HDIM)
    part = min(256, rows)

    for c in range(rows // part):
        cut = slice(c * part, (c + 1) * part)
        scores = (
            lax.dot_general(k_own, q_own[cut], NT, preferred_element_type=F32) * scale
        )
        key_pos = piece_row(iota((rows, part), 0), block_rows)
        query_pos = piece_row(iota((rows, part), 1) + c * part, block_rows)
        allowed = (lanes(id_own, part)[:, :part] == id_own_lane[0:1, cut]) & (key_pos <= query_pos)
        scores = jnp.where(allowed, scores, -jnp.inf)
        exponent = jnp.exp(scores - jnp.max(scores, axis=0, keepdims=True))
        probs[:, cut] = exponent * (1.0 / jnp.sum(exponent, axis=0, keepdims=True))

    @pl.when(half(me) == 0)
    def _():
        hand_out(1, half_tile(me), OWN_V)

    local = (id_own_lane - (CLUS_DEV * me).astype(F32)) == iota((8, rows), 0).astype(F32)
    cen_buf[head] = jnp.dot(onehot(local), k_own, preferred_element_type=F32)

    @pl.loop(1, n_head)
    def _(i):
        send_head(cen_buf.at[head], cen_buf.at[head], CEN, (head + i) % n_head)

    k_t[...] = k_own.astype(F32).T.astype(BF16)

    def await_half(first, remote, sem):
        @pl.when(half(me) == remote)
        def _():
            await_copy(own.at[1, pl.ds(first, pairs)], sem)

        @pl.when(half(me) == 1 - remote)
        def _():
            await_copy(own.at[1, pl.ds(first, pairs - 1)], sem)

    probs_low[...] = probs[...].astype(BF16)
    await_half(pairs, 0, recv_sem.at[OWN_G])
    g_own = own[1, pl.ds(pairs, pairs)].reshape(rows, HDIM)

    values_grad = jnp.dot(probs_low[...], g_own, preferred_element_type=F32)
    res[pl.ds(2 * pairs, pairs)] = values_grad.astype(BF16).reshape(pairs, TILE, HDIM)

    @pl.when(half(me) == 1)
    def _():
        mid1[1, me] = res[2 * pairs + half_tile(me)]

    @pl.loop(0, n_ctx - 1)
    def _(i):
        p = peer(i)

        @pl.when(half(p) == 1)
        def _():
            send(res.at[2 * pairs + half_tile(p)], mid1.at[1, me], GV, p)

    await_half(0, 1, recv_sem.at[OWN_V])
    v_own = own[1, pl.ds(0, pairs)].reshape(rows, HDIM)

    for c in range(rows // part):
        cut = slice(c * part, (c + 1) * part)
        dprob = lax.dot_general(v_own, g_own[cut], NT, preferred_element_type=F32)
        prob = probs[:, cut]
        delta = jnp.sum(probs_low[:, cut].astype(F32) * dprob, axis=0, keepdims=True)
        dscore[:, cut] = (prob * (dprob - delta)).astype(BF16)

    keys_grad = jnp.dot(dscore[...], q_own, preferred_element_type=F32) * scale
    res[pl.ds(pairs, pairs)] = keys_grad.astype(BF16).reshape(pairs, TILE, HDIM)
    queries_grad = jnp.dot(k_t[...], dscore[...], preferred_element_type=F32) * scale
    res[pl.ds(0, pairs)] = queries_grad.T.astype(BF16).reshape(pairs, TILE, HDIM)
    mid1[0, me] = res[me]

    @pl.loop(0, n_ctx - 1)
    def _(i):
        p = peer(i)
        send(res.at[p], mid1.at[0, me], GQK, p)

    @pl.when(half(me) == 1)
    def _():
        await_copy(mid1.at[1, pl.ds(0, n_ctx - 1)], recv_sem.at[GV])
        permute(unsort_mat, mid1, mid2, 1)
        back_v[half_tile(me)] = mid2[1, me]

        @pl.loop(0, n_ctx - 1)
        def _(i):
            p = peer(i)
            send(mid2.at[1, p], back_v.at[half_tile(me)], BACK_V, p)

    await_copy(mid1.at[0, pl.ds(0, n_ctx - 1)], recv_sem.at[GQK])
    permute(unsort_mat, mid1, mid2, 0)
    back[me] = mid2[0, me]

    @pl.loop(0, n_ctx - 1)
    def _(i):
        p = peer(i)
        send(mid2.at[0, p], back.at[me], BACK_QK, p)

    await_copy(cen_buf.at[pl.ds(0, n_head - 1)], recv_sem.at[CEN])
    whole = cen_buf[0]
    for h in range(1, n_head):
        whole = whole + cen_buf[h]
    centroids = whole / jnp.sqrt(jnp.mean(whole * whole, axis=1, keepdims=True) + 1e-06)
    cen_own[...] = centroids[:CLUS_DEV]
    store_cen = pltpu.make_async_copy(cen_own, cen_ref, load_sem.at[1])
    store_cen.start()

    @pl.when(half(me) == 1)
    def _():
        await_copy(back_v.at[pl.ds(0, pairs - 1)], recv_sem.at[BACK_V])
        await_copy(res.at[pl.ds(2 * pairs, pairs - 1)], send_sem.at[GV])
        await_copy(mid2.at[1, pl.ds(0, n_ctx - 1)], send_sem.at[BACK_V])

    @pl.when(half(me) == 0)
    def _():
        await_copy(back_v.at[pl.ds(0, pairs)], recv_sem.at[BACK_V])
        await_copy(res.at[pl.ds(2 * pairs, pairs)], send_sem.at[GV])

    unpack([back_v[...]], [dv_own])
    store_dv = pltpu.make_async_copy(dv_own, dv_ref, load_sem.at[2])
    store_dv.start()
    groups = n_ctx // n_head

    @pl.when(collects)
    def _():
        await_copy(ids_all.at[pl.ds(0, groups - 1)], send_sem.at[IDS])

        @pl.loop(1, n_head)
        def _(i):
            await_copy(ids_all, send_sem.at[SHARE])

    @pl.when(jnp.logical_not(collects))
    def _():
        await_copy(ids_all.at[pl.ds(0, groups)], send_sem.at[IDS])

    await_copy(pack.at[pl.ds(0, n_ctx - 1)], send_sem.at[IN_A])
    await_copy(pack.at[pl.ds(0, n_ctx - 1)], send_sem.at[IN_B])
    await_copy(in2.at[0, pl.ds(0, n_ctx - 1)], send_sem.at[OWN_A])
    await_copy(in2.at[1, pl.ds(0, n_ctx - 1)], send_sem.at[OWN_V + half(me)])
    await_copy(res.at[pl.ds(0, n_ctx - 1)], send_sem.at[GQK])
    await_copy(mid2.at[0, pl.ds(0, n_ctx - 1)], send_sem.at[BACK_QK])
    await_copy(cen_buf.at[pl.ds(0, n_head - 1)], send_sem.at[CEN])
    store_cen.wait()
    store_dv.wait()
    await_copy(back.at[pl.ds(0, n_ctx - 1)], recv_sem.at[BACK_QK])


def finish(back, dv_in, cen_in, dq_out, dk_out, dv_out, cen_out, tiles, grads, cen, load, store):
    pairs = back.shape[0] // 2
    loads = [
        pltpu.make_async_copy(back.at[pl.ds(0, pairs)], tiles.at[0], load.at[0]),
        pltpu.make_async_copy(back.at[pl.ds(pairs, pairs)], tiles.at[1], load.at[1]),
        pltpu.make_async_copy(dv_in, grads.at[2], load.at[2]),
        pltpu.make_async_copy(cen_in, cen, load.at[3]),
    ]
    stores = [
        pltpu.make_async_copy(grads.at[0], dq_out, store.at[0]),
        pltpu.make_async_copy(grads.at[1], dk_out, store.at[1]),
        pltpu.make_async_copy(grads.at[2], dv_out, store.at[2]),
        pltpu.make_async_copy(cen, cen_out, store.at[3]),
    ]
    for copy in loads:
        copy.start()
    loads[0].wait()
    loads[1].wait()
    unpack([tiles[0], tiles[1]], [grads.at[0], grads.at[1]])
    for a in range(4):
        if a > 1:
            loads[a].wait()
        stores[a].start()
    for copy in stores:
        copy.wait()


def shards(queries, keys, values, out_grad, cluster_ids):
    n_ctx, n_head = lax.axis_size("ctx"), lax.axis_size("head")
    rows = queries.shape[0]
    pairs, grows = n_ctx // 2, TILE * n_ctx
    vmem = pl.BlockSpec(memory_space=pltpu.VMEM)
    hbm = pl.BlockSpec(memory_space=pltpu.HBM)
    grad = jax.ShapeDtypeStruct((rows, HDIM), BF16)
    centroid = jax.ShapeDtypeStruct((CLUS_DEV, HDIM), F32)
    back, dv, cen = pl.pallas_call(
        functools.partial(kernel, n_ctx, n_head),
        out_shape=(jax.ShapeDtypeStruct((n_ctx, TILE, HDIM), BF16), grad, centroid),
        in_specs=[hbm] * 5,
        out_specs=(vmem, hbm, hbm),
        scratch_shapes=[
            pltpu.VMEM((4, rows, HDIM), BF16),
            pltpu.SMEM((BLOCKS,), jnp.int32),
            pltpu.VMEM((1, HDIM), F32),
            pltpu.VMEM((4 * pairs, TILE, HDIM), BF16),
            pltpu.VMEM((n_ctx, 1, HDIM), F32),
            pltpu.VMEM((grows, HDIM), F32),
            pltpu.VMEM((2, n_ctx, TILE, HDIM), BF16),
            pltpu.VMEM((2, n_ctx, TILE, HDIM), BF16),
            pltpu.VMEM((2, n_ctx, TILE, HDIM), BF16),
            pltpu.VMEM((3 * pairs, TILE, HDIM), BF16),
            pltpu.VMEM((2, n_ctx, TILE, HDIM), BF16),
            pltpu.VMEM((2, n_ctx, TILE, HDIM), BF16),
            pltpu.VMEM((pairs, TILE, HDIM), BF16),
            pltpu.VMEM((grows, grows), BF16),
            pltpu.VMEM((grows, grows), BF16),
            pltpu.VMEM((rows, rows), F32),
            pltpu.VMEM((rows, rows), BF16),
            pltpu.VMEM((rows, rows), BF16),
            pltpu.VMEM((HDIM, rows), BF16),
            pltpu.VMEM((n_head, 8, HDIM), F32),
            pltpu.VMEM((CLUS_DEV, HDIM), F32),
            pltpu.VMEM((rows, HDIM), BF16),
            pltpu.SemaphoreType.DMA((5,)),
            pltpu.SemaphoreType.DMA((12,)),
            pltpu.SemaphoreType.DMA((12,)),
        ],
        compiler_params=pltpu.CompilerParams(
            collective_id=0, has_side_effects=True
        ),
        name="routing_attention",
    )(queries, keys, values, out_grad, cluster_ids)
    return pl.pallas_call(
        finish,
        out_shape=(grad, grad, grad, centroid),
        in_specs=[hbm] * 3,
        out_specs=(hbm,) * 4,
        scratch_shapes=[
            pltpu.VMEM((2, pairs, TILE, HDIM), BF16),
            pltpu.VMEM((3, rows, HDIM), BF16),
            pltpu.VMEM((CLUS_DEV, HDIM), F32),
            pltpu.SemaphoreType.DMA((4,)),
            pltpu.SemaphoreType.DMA((4,)),
        ],
        name="finish",
    )(back, dv, cen)


def solution(mesh):
    placed = (P("ctx", "head"), P("ctx", "head"), P("ctx", "head"), P("ctx", "head"), P("ctx"))
    return jax.shard_map(
        shards,
        mesh=mesh,
        in_specs=placed,
        out_specs=(P("ctx", "head"), P("ctx", "head"), P("ctx", "head"), P("ctx", None)),
        check_vma=False,
    )
```

```python
import functools
import math

import jax
import jax.numpy as jnp
from jax import lax
from jax.experimental import pallas as pl
from jax.experimental.pallas import tpu as pltpu
from jax.sharding import PartitionSpec as P

HDIM = 128
CLUS_DEV = 4
BLOCKS = 8
TILE = 16
RING_Y = 4
MESH = pl.DeviceIdType.MESH
NT = (((1,), (1,)), ((), ()))
F32 = jnp.float32
BF16 = jnp.bfloat16

IDS, IN_A, IN_B, OWN_A, OWN_V, OWN_G, GV, GQK, BACK_V, BACK_QK, CEN, SHARE = range(12)


def iota(shape, dim):
    return lax.broadcasted_iota(jnp.int32, shape, dim)


def onehot(mask):
    return jnp.where(mask, 1.0, 0.0).astype(BF16)


def piece_row(r, block_rows):
    return ((r >> 1) & (BLOCKS - 1)) * block_rows + 2 * (r >> 4) + (r & 1)


def lanes(column, width):
    return jnp.concatenate([column] * (width // HDIM), axis=1) if width > HDIM else column


def unpack(tiles, outs):
    rows = tiles[0].shape[0] * TILE
    data = jnp.concatenate([t.reshape(rows, HDIM) for t in tiles], axis=1)
    chunk = min(256, rows)
    for c in range(rows // chunk):
        source = piece_row(iota((chunk, rows), 1), rows // BLOCKS)
        picked = jnp.dot(
            onehot(source == iota((chunk, rows), 0) + c * chunk), data,
            preferred_element_type=F32,
        ).astype(BF16)
        for a, out in enumerate(outs):
            out[pl.ds(c * chunk, chunk), :] = picked[:, a * HDIM : (a + 1) * HDIM]


def kernel(
    n_ctx, n_head,
    q_ref, k_ref, v_ref, g_ref, id_ref,
    back, dv_ref, cen_ref,
    staged, id_words, id_row, pack, ids_all, idc, in1, in2, own, res, mid1, mid2, back_v,
    sort_mat, unsort_mat, probs, probs_low, dscore, k_t, cen_buf, cen_own, dv_own, load_sem, send_sem, recv_sem,
):
    me = lax.axis_index("ctx")
    head = lax.axis_index("head")
    core = head % 2
    my_z, my_y = me // RING_Y, me % RING_Y
    n_z = n_ctx // RING_Y
    pairs = n_ctx // 2
    rows = BLOCKS * n_ctx
    grows = TILE * n_ctx
    block_rows = n_ctx
    scale = 1.0 / math.sqrt(HDIM)

    def peer(i):
        odd, step = lax.rem(i, 2), lax.div(i, 8)
        dz = n_z // 2 + step - odd * (2 * step + 1)
        dy = lax.div(i, 2) + 1
        return lax.rem(my_z + dz, n_z) * RING_Y + lax.rem(my_y + dy, RING_Y)

    def half_tile(p):
        return lax.div(p, 2 * RING_Y) * RING_Y + lax.rem(p, RING_Y)

    def half(p):
        return lax.rem(lax.div(p, RING_Y) + core + 1, 2)

    def send(src, dst, phase, p):
        pltpu.make_async_remote_copy(
            src_ref=src, dst_ref=dst, send_sem=send_sem.at[phase], recv_sem=recv_sem.at[phase],
            device_id={"ctx": p}, device_id_type=MESH,
        ).start()

    def send_head(src, dst, phase, h):
        pltpu.make_async_remote_copy(
            src_ref=src, dst_ref=dst, send_sem=send_sem.at[phase], recv_sem=recv_sem.at[phase],
            device_id={"head": h}, device_id_type=MESH,
        ).start()

    def await_copy(ref, sem):
        pltpu.make_async_copy(ref, ref, sem).wait()

    barrier = pltpu.get_barrier_semaphore()

    @pl.loop(0, n_ctx - 1)
    def _(i):
        pl.semaphore_signal(barrier, 1, device_id={"ctx": peer(i)}, device_id_type=MESH)

    @pl.loop(1, n_head)
    def _(i):
        pl.semaphore_signal(
            barrier, 1, device_id={"head": (head + i) % n_head}, device_id_type=MESH
        )

    loads = [
        pltpu.make_async_copy(ref, staged.at[a], load_sem.at[a])
        for a, ref in enumerate((q_ref, k_ref, v_ref, g_ref))
    ] + [pltpu.make_async_copy(id_ref, id_words, load_sem.at[4])]
    for load in loads:
        load.start()
    for load in loads:
        load.wait()

    chunk = min(128, rows)
    every = jnp.concatenate([staged[a] for a in range(4)], axis=1)

    @pl.loop(0, rows // chunk)
    def _(c):
        source = piece_row(iota((chunk, rows), 0) + c * chunk, block_rows)
        picked = jnp.dot(
            onehot(source == iota((chunk, rows), 1)), every, preferred_element_type=F32
        ).astype(BF16)
        tiles = chunk // TILE
        for a in range(4):
            pack[pl.ds(a * pairs + c * tiles, tiles)] = picked[
                :, a * HDIM : (a + 1) * HDIM
            ].reshape(tiles, TILE, HDIM)

    words = jnp.zeros((1, HDIM), jnp.int32)
    for b in range(BLOCKS):
        words = jnp.where(iota((1, HDIM), 1) == b, id_words[b], words)
    id_row[...] = words.astype(F32)
    collects = me % n_head == head

    @pl.when(collects)
    def _():
        ids_all[me] = id_row[...]


    def second(p):
        return n_ctx + half(p) * pairs + half_tile(p)

    in1[0, me] = pack[me]
    in1[1, me] = pack[second(me)]

    pl.semaphore_wait(barrier, n_ctx - 1 + n_head - 1)

    @pl.loop(0, n_ctx // n_head)
    def _(i):
        p = i * n_head + head

        @pl.when(p != me)
        def _():
            send(id_row, ids_all.at[me], IDS, p)

    @pl.loop(0, n_ctx - 1)
    def _(i):
        p = peer(i)
        send(pack.at[p], in1.at[0, me], IN_A, p)

    @pl.loop(0, n_ctx - 1)
    def _(i):
        p = peer(i)
        send(pack.at[second(p)], in1.at[1, me], IN_B, p)

    @pl.when(collects)
    def _():
        await_copy(ids_all.at[pl.ds(0, n_ctx - 1)], recv_sem.at[IDS])

        @pl.loop(1, n_head)
        def _(i):
            send_head(ids_all, ids_all, SHARE, (head + i) % n_head)

    @pl.when(jnp.logical_not(collects))
    def _():
        await_copy(ids_all, recv_sem.at[SHARE])

    id_rows = ids_all[...].reshape(n_ctx, HDIM).astype(BF16)
    spread = jnp.dot(
        onehot((iota((grows, n_ctx), 0) >> 4) == iota((grows, n_ctx), 1)),
        id_rows, preferred_element_type=F32,
    )
    keep = ((iota((grows, HDIM), 0) >> 1) & (BLOCKS - 1)) == iota((grows, HDIM), 1)
    spread = jnp.where(keep, spread, 0.0).astype(BF16)
    idc[...] = jnp.dot(spread, jnp.ones((HDIM, HDIM), BF16), preferred_element_type=F32)
    id_lane = lax.dot_general(jnp.ones((8, HDIM), BF16), spread, NT, preferred_element_type=F32)
    owner_lane = jnp.floor(id_lane[0:1] * (1.0 / CLUS_DEV))

    step = min(128, grows)

    def rank(c, before):
        owner = jnp.floor(idc[pl.ds(c * step, step), :] * (1.0 / CLUS_DEV))
        same = lanes(owner, grows) == owner_lane
        row = (iota((step, grows), 0) + c * step) >> 1
        column = iota((step, grows), 1) >> 1
        before = before + jnp.sum(
            jnp.where(same & (row < column), 1.0, 0.0), axis=0, keepdims=True
        )
        ahead = jnp.dot(
            onehot(same & (column < row)), jnp.ones((grows, HDIM), BF16),
            preferred_element_type=F32,
        )
        parity = (iota((step, HDIM), 0) & 1).astype(F32)
        place = TILE * owner + ahead + parity
        unsort_mat[pl.ds(c * step, step), :] = onehot(
            lanes(place, grows) == iota((step, grows), 1).astype(F32)
        )
        return before

    before = lax.fori_loop(0, grows // step, rank, jnp.zeros((1, grows), F32))
    place_lane = TILE * owner_lane + before + (iota((1, grows), 1) & 1).astype(F32)

    @pl.loop(0, grows // step)
    def _(c):
        row = (iota((step, grows), 0) + c * step).astype(F32)
        sort_mat[pl.ds(c * step, step), :] = onehot(row == place_lane)

    id_tile = jnp.dot(
        sort_mat[pl.ds(pl.multiple_of(me * TILE, TILE), TILE), :], idc[...].astype(BF16),
        preferred_element_type=F32,
    )
    id_own = jnp.concatenate([id_tile] * pairs, axis=0)
    id_own_lane = lax.dot_general(
        onehot(iota((8, HDIM), 1) == 0), id_own.astype(BF16), NT, preferred_element_type=F32
    )

    wide = min(256, grows)

    def permute(mat, src, dst, which):
        data = src[which].reshape(grows, HDIM)

        @pl.loop(0, grows // wide)
        def _(c):
            moved = jnp.dot(
                mat[pl.ds(c * wide, wide), :], data, preferred_element_type=F32
            ).astype(BF16)
            dst[which, pl.ds(c * (wide // TILE), wide // TILE)] = moved.reshape(
                wide // TILE, TILE, HDIM
            )

    def hand_out(which, slot, phase):
        own[which, slot] = in2[which, me]

        @pl.loop(0, n_ctx - 1)
        def _(i):
            p = peer(i)
            send(in2.at[which, p], own.at[which, slot], phase, p)

    await_copy(in1.at[0, pl.ds(0, n_ctx - 1)], recv_sem.at[IN_A])
    permute(sort_mat, in1, in2, 0)
    hand_out(0, me, OWN_A)
    await_copy(in1.at[1, pl.ds(0, n_ctx - 1)], recv_sem.at[IN_B])
    permute(sort_mat, in1, in2, 1)

    @pl.when(half(me) == 1)
    def _():
        hand_out(1, pairs + half_tile(me), OWN_G)

    await_copy(own.at[0, pl.ds(0, n_ctx - 1)], recv_sem.at[OWN_A])
    q_own = own[0, pl.ds(0, pairs)].reshape(rows, HDIM)
    k_own = own[0, pl.ds(pairs, pairs)].reshape(rows, HDIM)
    part = min(256, rows)

    for c in range(rows // part):
        cut = slice(c * part, (c + 1) * part)
        scores = (
            lax.dot_general(k_own, q_own[cut], NT, preferred_element_type=F32) * scale
        )
        key_pos = piece_row(iota((rows, part), 0), block_rows)
        query_pos = piece_row(iota((rows, part), 1) + c * part, block_rows)
        allowed = (lanes(id_own, part)[:, :part] == id_own_lane[0:1, cut]) & (key_pos <= query_pos)
        scores = jnp.where(allowed, scores, -jnp.inf)
        exponent = jnp.exp(scores - jnp.max(scores, axis=0, keepdims=True))
        probs[:, cut] = exponent * (1.0 / jnp.sum(exponent, axis=0, keepdims=True))

    @pl.when(half(me) == 0)
    def _():
        hand_out(1, half_tile(me), OWN_V)

    local = (id_own_lane - (CLUS_DEV * me).astype(F32)) == iota((8, rows), 0).astype(F32)
    cen_buf[head] = jnp.dot(onehot(local), k_own, preferred_element_type=F32)

    @pl.loop(1, n_head)
    def _(i):
        send_head(cen_buf.at[head], cen_buf.at[head], CEN, (head + i) % n_head)

    k_t[...] = k_own.astype(F32).T.astype(BF16)

    def await_half(first, remote, sem):
        @pl.when(half(me) == remote)
        def _():
            await_copy(own.at[1, pl.ds(first, pairs)], sem)

        @pl.when(half(me) == 1 - remote)
        def _():
            await_copy(own.at[1, pl.ds(first, pairs - 1)], sem)

    probs_low[...] = probs[...].astype(BF16)
    await_half(pairs, 0, recv_sem.at[OWN_G])
    g_own = own[1, pl.ds(pairs, pairs)].reshape(rows, HDIM)

    values_grad = jnp.dot(probs_low[...], g_own, preferred_element_type=F32)
    res[pl.ds(2 * pairs, pairs)] = values_grad.astype(BF16).reshape(pairs, TILE, HDIM)

    @pl.when(half(me) == 1)
    def _():
        mid1[1, me] = res[2 * pairs + half_tile(me)]

    @pl.loop(0, n_ctx - 1)
    def _(i):
        p = peer(i)

        @pl.when(half(p) == 1)
        def _():
            send(res.at[2 * pairs + half_tile(p)], mid1.at[1, me], GV, p)

    await_half(0, 1, recv_sem.at[OWN_V])
    v_own = own[1, pl.ds(0, pairs)].reshape(rows, HDIM)

    for c in range(rows // part):
        cut = slice(c * part, (c + 1) * part)
        dprob = lax.dot_general(v_own, g_own[cut], NT, preferred_element_type=F32)
        prob = probs[:, cut]
        delta = jnp.sum(probs_low[:, cut].astype(F32) * dprob, axis=0, keepdims=True)
        dscore[:, cut] = (prob * (dprob - delta)).astype(BF16)

    keys_grad = jnp.dot(dscore[...], q_own, preferred_element_type=F32) * scale
    res[pl.ds(pairs, pairs)] = keys_grad.astype(BF16).reshape(pairs, TILE, HDIM)
    queries_grad = jnp.dot(k_t[...], dscore[...], preferred_element_type=F32) * scale
    res[pl.ds(0, pairs)] = queries_grad.T.astype(BF16).reshape(pairs, TILE, HDIM)
    mid1[0, me] = res[me]

    @pl.loop(0, n_ctx - 1)
    def _(i):
        p = peer(i)
        send(res.at[p], mid1.at[0, me], GQK, p)

    @pl.when(half(me) == 1)
    def _():
        await_copy(mid1.at[1, pl.ds(0, n_ctx - 1)], recv_sem.at[GV])
        permute(unsort_mat, mid1, mid2, 1)
        back_v[half_tile(me)] = mid2[1, me]

        @pl.loop(0, n_ctx - 1)
        def _(i):
            p = peer(i)
            send(mid2.at[1, p], back_v.at[half_tile(me)], BACK_V, p)

    await_copy(mid1.at[0, pl.ds(0, n_ctx - 1)], recv_sem.at[GQK])
    permute(unsort_mat, mid1, mid2, 0)
    back[me] = mid2[0, me]

    @pl.loop(0, n_ctx - 1)
    def _(i):
        p = peer(i)
        send(mid2.at[0, p], back.at[me], BACK_QK, p)

    await_copy(cen_buf.at[pl.ds(0, n_head - 1)], recv_sem.at[CEN])
    whole = cen_buf[0]
    for h in range(1, n_head):
        whole = whole + cen_buf[h]
    centroids = whole / jnp.sqrt(jnp.mean(whole * whole, axis=1, keepdims=True) + 1e-06)
    cen_own[...] = centroids[:CLUS_DEV]
    store_cen = pltpu.make_async_copy(cen_own, cen_ref, load_sem.at[1])
    store_cen.start()

    @pl.when(half(me) == 1)
    def _():
        await_copy(back_v.at[pl.ds(0, pairs - 1)], recv_sem.at[BACK_V])
        await_copy(res.at[pl.ds(2 * pairs, pairs - 1)], send_sem.at[GV])
        await_copy(mid2.at[1, pl.ds(0, n_ctx - 1)], send_sem.at[BACK_V])

    @pl.when(half(me) == 0)
    def _():
        await_copy(back_v.at[pl.ds(0, pairs)], recv_sem.at[BACK_V])
        await_copy(res.at[pl.ds(2 * pairs, pairs)], send_sem.at[GV])

    unpack([back_v[...]], [dv_own])
    store_dv = pltpu.make_async_copy(dv_own, dv_ref, load_sem.at[2])
    store_dv.start()
    groups = n_ctx // n_head

    @pl.when(collects)
    def _():
        await_copy(ids_all.at[pl.ds(0, groups - 1)], send_sem.at[IDS])

        @pl.loop(1, n_head)
        def _(i):
            await_copy(ids_all, send_sem.at[SHARE])

    @pl.when(jnp.logical_not(collects))
    def _():
        await_copy(ids_all.at[pl.ds(0, groups)], send_sem.at[IDS])

    await_copy(pack.at[pl.ds(0, n_ctx - 1)], send_sem.at[IN_A])
    await_copy(pack.at[pl.ds(0, n_ctx - 1)], send_sem.at[IN_B])
    await_copy(in2.at[0, pl.ds(0, n_ctx - 1)], send_sem.at[OWN_A])
    await_copy(in2.at[1, pl.ds(0, n_ctx - 1)], send_sem.at[OWN_V + half(me)])
    await_copy(res.at[pl.ds(0, n_ctx - 1)], send_sem.at[GQK])
    await_copy(mid2.at[0, pl.ds(0, n_ctx - 1)], send_sem.at[BACK_QK])
    await_copy(cen_buf.at[pl.ds(0, n_head - 1)], send_sem.at[CEN])
    store_cen.wait()
    store_dv.wait()
    await_copy(back.at[pl.ds(0, n_ctx - 1)], recv_sem.at[BACK_QK])


def finish(back, dv_in, cen_in, dq_out, dk_out, dv_out, cen_out, tiles, grads, cen, load, store):
    pairs = back.shape[0] // 2
    loads = [
        pltpu.make_async_copy(back.at[pl.ds(0, pairs)], tiles.at[0], load.at[0]),
        pltpu.make_async_copy(back.at[pl.ds(pairs, pairs)], tiles.at[1], load.at[1]),
        pltpu.make_async_copy(dv_in, grads.at[2], load.at[2]),
        pltpu.make_async_copy(cen_in, cen, load.at[3]),
    ]
    stores = [
        pltpu.make_async_copy(grads.at[0], dq_out, store.at[0]),
        pltpu.make_async_copy(grads.at[1], dk_out, store.at[1]),
        pltpu.make_async_copy(grads.at[2], dv_out, store.at[2]),
        pltpu.make_async_copy(cen, cen_out, store.at[3]),
    ]
    for copy in loads:
        copy.start()
    loads[0].wait()
    loads[1].wait()
    unpack([tiles[0], tiles[1]], [grads.at[0], grads.at[1]])
    for a in range(4):
        if a > 1:
            loads[a].wait()
        stores[a].start()
    for copy in stores:
        copy.wait()


def shards(queries, keys, values, out_grad, cluster_ids):
    n_ctx, n_head = lax.axis_size("ctx"), lax.axis_size("head")
    rows = queries.shape[0]
    pairs, grows = n_ctx // 2, TILE * n_ctx
    vmem = pl.BlockSpec(memory_space=pltpu.VMEM)
    hbm = pl.BlockSpec(memory_space=pltpu.HBM)
    grad = jax.ShapeDtypeStruct((rows, HDIM), BF16)
    centroid = jax.ShapeDtypeStruct((CLUS_DEV, HDIM), F32)
    back, dv, cen = pl.pallas_call(
        functools.partial(kernel, n_ctx, n_head),
        out_shape=(jax.ShapeDtypeStruct((n_ctx, TILE, HDIM), BF16), grad, centroid),
        in_specs=[hbm] * 5,
        out_specs=(vmem, hbm, hbm),
        scratch_shapes=[
            pltpu.VMEM((4, rows, HDIM), BF16),
            pltpu.SMEM((BLOCKS,), jnp.int32),
            pltpu.VMEM((1, HDIM), F32),
            pltpu.VMEM((4 * pairs, TILE, HDIM), BF16),
            pltpu.VMEM((n_ctx, 1, HDIM), F32),
            pltpu.VMEM((grows, HDIM), F32),
            pltpu.VMEM((2, n_ctx, TILE, HDIM), BF16),
            pltpu.VMEM((2, n_ctx, TILE, HDIM), BF16),
            pltpu.VMEM((2, n_ctx, TILE, HDIM), BF16),
            pltpu.VMEM((3 * pairs, TILE, HDIM), BF16),
            pltpu.VMEM((2, n_ctx, TILE, HDIM), BF16),
            pltpu.VMEM((2, n_ctx, TILE, HDIM), BF16),
            pltpu.VMEM((pairs, TILE, HDIM), BF16),
            pltpu.VMEM((grows, grows), BF16),
            pltpu.VMEM((grows, grows), BF16),
            pltpu.VMEM((rows, rows), F32),
            pltpu.VMEM((rows, rows), BF16),
            pltpu.VMEM((rows, rows), BF16),
            pltpu.VMEM((HDIM, rows), BF16),
            pltpu.VMEM((n_head, 8, HDIM), F32),
            pltpu.VMEM((CLUS_DEV, HDIM), F32),
            pltpu.VMEM((rows, HDIM), BF16),
            pltpu.SemaphoreType.DMA((5,)),
            pltpu.SemaphoreType.DMA((12,)),
            pltpu.SemaphoreType.DMA((12,)),
        ],
        compiler_params=pltpu.CompilerParams(
            collective_id=0, has_side_effects=True
        ),
        name="routing_attention",
    )(queries, keys, values, out_grad, cluster_ids)
    return pl.pallas_call(
        finish,
        out_shape=(grad, grad, grad, centroid),
        in_specs=[hbm] * 3,
        out_specs=(hbm,) * 4,
        scratch_shapes=[
            pltpu.VMEM((2, pairs, TILE, HDIM), BF16),
            pltpu.VMEM((3, rows, HDIM), BF16),
            pltpu.VMEM((CLUS_DEV, HDIM), F32),
            pltpu.SemaphoreType.DMA((4,)),
            pltpu.SemaphoreType.DMA((4,)),
        ],
        name="finish",
    )(back, dv, cen)


def solution(mesh):
    placed = (P("ctx", "head"), P("ctx", "head"), P("ctx", "head"), P("ctx", "head"), P("ctx"))
    return jax.shard_map(
        shards,
        mesh=mesh,
        in_specs=placed,
        out_specs=(P("ctx", "head"), P("ctx", "head"), P("ctx", "head"), P("ctx", None)),
        check_vma=False,
    )
```

```python
import functools
import math

import jax
import jax.numpy as jnp
from jax import lax
from jax.experimental import pallas as pl
from jax.experimental.pallas import tpu as pltpu
from jax.sharding import PartitionSpec as P

HDIM = 128
CLUS_DEV = 4
BLOCKS = 8
TILE = 16
RING_Y = 4
MESH = pl.DeviceIdType.MESH
NT = (((1,), (1,)), ((), ()))
F32 = jnp.float32
BF16 = jnp.bfloat16

IDS, IN_A, IN_B, OWN_A, OWN_V, OWN_G, GV, GQK, BACK_V, BACK_QK, CEN, SHARE = range(12)


def iota(shape, dim):
    return lax.broadcasted_iota(jnp.int32, shape, dim)


def onehot(mask):
    return jnp.where(mask, 1.0, 0.0).astype(BF16)


def piece_row(r, block_rows):
    return ((r >> 1) & (BLOCKS - 1)) * block_rows + 2 * (r >> 4) + (r & 1)


def lanes(column, width):
    return jnp.concatenate([column] * (width // HDIM), axis=1) if width > HDIM else column


def unpack(tiles, outs):
    rows = tiles[0].shape[0] * TILE
    data = jnp.concatenate([t.reshape(rows, HDIM) for t in tiles], axis=1)
    chunk = min(256, rows)
    for c in range(rows // chunk):
        source = piece_row(iota((chunk, rows), 1), rows // BLOCKS)
        picked = jnp.dot(
            onehot(source == iota((chunk, rows), 0) + c * chunk), data,
            preferred_element_type=F32,
        ).astype(BF16)
        for a, out in enumerate(outs):
            out[pl.ds(c * chunk, chunk), :] = picked[:, a * HDIM : (a + 1) * HDIM]


def kernel(
    n_ctx, n_head,
    q_ref, k_ref, v_ref, g_ref, id_ref,
    back, dv_ref, cen_ref,
    staged, id_words, id_row, pack, ids_all, idc, in1, in2, own, res, mid1, mid2, back_v,
    sort_mat, unsort_mat, probs, probs_low, dscore, k_t, cen_buf, cen_own, dv_own, load_sem, send_sem, recv_sem,
):
    me = lax.axis_index("ctx")
    head = lax.axis_index("head")
    core = head % 2
    my_z, my_y = me // RING_Y, me % RING_Y
    n_z = n_ctx // RING_Y
    pairs = n_ctx // 2
    rows = BLOCKS * n_ctx
    grows = TILE * n_ctx
    block_rows = n_ctx
    scale = 1.0 / math.sqrt(HDIM)

    def peer(i):
        odd, step = lax.rem(i, 2), lax.div(i, 8)
        dz = n_z // 2 + step - odd * (2 * step + 1)
        dy = lax.div(i, 2) + 1
        return lax.rem(my_z + dz, n_z) * RING_Y + lax.rem(my_y + dy, RING_Y)

    def half_tile(p):
        return lax.div(p, 2 * RING_Y) * RING_Y + lax.rem(p, RING_Y)

    def half(p):
        return lax.rem(lax.div(p, RING_Y) + core + 1, 2)

    def send(src, dst, phase, p):
        pltpu.make_async_remote_copy(
            src_ref=src, dst_ref=dst, send_sem=send_sem.at[phase], recv_sem=recv_sem.at[phase],
            device_id={"ctx": p}, device_id_type=MESH,
        ).start()

    def send_head(src, dst, phase, h):
        pltpu.make_async_remote_copy(
            src_ref=src, dst_ref=dst, send_sem=send_sem.at[phase], recv_sem=recv_sem.at[phase],
            device_id={"head": h}, device_id_type=MESH,
        ).start()

    def await_copy(ref, sem):
        pltpu.make_async_copy(ref, ref, sem).wait()

    barrier = pltpu.get_barrier_semaphore()

    @pl.loop(0, n_ctx - 1)
    def _(i):
        pl.semaphore_signal(barrier, 1, device_id={"ctx": peer(i)}, device_id_type=MESH)

    @pl.loop(1, n_head)
    def _(i):
        pl.semaphore_signal(
            barrier, 1, device_id={"head": (head + i) % n_head}, device_id_type=MESH
        )

    loads = [
        pltpu.make_async_copy(ref, staged.at[a], load_sem.at[a])
        for a, ref in enumerate((q_ref, k_ref, v_ref, g_ref))
    ] + [pltpu.make_async_copy(id_ref, id_words, load_sem.at[4])]
    for load in loads:
        load.start()
    for a in (0, 1, 4):
        loads[a].wait()

    chunk = min(128, rows)

    def pack_two(first):
        every = jnp.concatenate([staged[first], staged[first + 1]], axis=1)

        @pl.loop(0, rows // chunk)
        def _(c):
            source = piece_row(iota((chunk, rows), 0) + c * chunk, block_rows)
            picked = jnp.dot(
                onehot(source == iota((chunk, rows), 1)), every, preferred_element_type=F32
            ).astype(BF16)
            tiles = chunk // TILE
            for a in range(2):
                pack[pl.ds((first + a) * pairs + c * tiles, tiles)] = picked[
                    :, a * HDIM : (a + 1) * HDIM
                ].reshape(tiles, TILE, HDIM)

    pack_two(0)
    words = jnp.zeros((1, HDIM), jnp.int32)
    for b in range(BLOCKS):
        words = jnp.where(iota((1, HDIM), 1) == b, id_words[b], words)
    id_row[...] = words.astype(F32)
    collects = me % n_head == head

    @pl.when(collects)
    def _():
        ids_all[me] = id_row[...]


    def second(p):
        return n_ctx + half(p) * pairs + half_tile(p)

    in1[0, me] = pack[me]

    pl.semaphore_wait(barrier, n_ctx - 1 + n_head - 1)

    @pl.loop(0, n_ctx // n_head)
    def _(i):
        p = i * n_head + head

        @pl.when(p != me)
        def _():
            send(id_row, ids_all.at[me], IDS, p)

    @pl.loop(0, n_ctx - 1)
    def _(i):
        p = peer(i)
        send(pack.at[p], in1.at[0, me], IN_A, p)

    loads[2].wait()
    loads[3].wait()
    pack_two(2)
    in1[1, me] = pack[second(me)]

    @pl.loop(0, n_ctx - 1)
    def _(i):
        p = peer(i)
        send(pack.at[second(p)], in1.at[1, me], IN_B, p)

    @pl.when(collects)
    def _():
        await_copy(ids_all.at[pl.ds(0, n_ctx - 1)], recv_sem.at[IDS])

        @pl.loop(1, n_head)
        def _(i):
            send_head(ids_all, ids_all, SHARE, (head + i) % n_head)

    @pl.when(jnp.logical_not(collects))
    def _():
        await_copy(ids_all, recv_sem.at[SHARE])

    id_rows = ids_all[...].reshape(n_ctx, HDIM).astype(BF16)
    spread = jnp.dot(
        onehot((iota((grows, n_ctx), 0) >> 4) == iota((grows, n_ctx), 1)),
        id_rows, preferred_element_type=F32,
    )
    keep = ((iota((grows, HDIM), 0) >> 1) & (BLOCKS - 1)) == iota((grows, HDIM), 1)
    spread = jnp.where(keep, spread, 0.0).astype(BF16)
    idc[...] = jnp.dot(spread, jnp.ones((HDIM, HDIM), BF16), preferred_element_type=F32)
    id_lane = lax.dot_general(jnp.ones((8, HDIM), BF16), spread, NT, preferred_element_type=F32)
    owner_lane = jnp.floor(id_lane[0:1] * (1.0 / CLUS_DEV))

    step = min(128, grows)

    def rank(c, before):
        owner = jnp.floor(idc[pl.ds(c * step, step), :] * (1.0 / CLUS_DEV))
        same = lanes(owner, grows) == owner_lane
        row = (iota((step, grows), 0) + c * step) >> 1
        column = iota((step, grows), 1) >> 1
        before = before + jnp.sum(
            jnp.where(same & (row < column), 1.0, 0.0), axis=0, keepdims=True
        )
        ahead = jnp.dot(
            onehot(same & (column < row)), jnp.ones((grows, HDIM), BF16),
            preferred_element_type=F32,
        )
        parity = (iota((step, HDIM), 0) & 1).astype(F32)
        place = TILE * owner + ahead + parity
        unsort_mat[pl.ds(c * step, step), :] = onehot(
            lanes(place, grows) == iota((step, grows), 1).astype(F32)
        )
        return before

    before = lax.fori_loop(0, grows // step, rank, jnp.zeros((1, grows), F32))
    place_lane = TILE * owner_lane + before + (iota((1, grows), 1) & 1).astype(F32)

    @pl.loop(0, grows // step)
    def _(c):
        row = (iota((step, grows), 0) + c * step).astype(F32)
        sort_mat[pl.ds(c * step, step), :] = onehot(row == place_lane)

    id_tile = jnp.dot(
        sort_mat[pl.ds(pl.multiple_of(me * TILE, TILE), TILE), :], idc[...].astype(BF16),
        preferred_element_type=F32,
    )
    id_own = jnp.concatenate([id_tile] * pairs, axis=0)
    id_own_lane = lax.dot_general(
        onehot(iota((8, HDIM), 1) == 0), id_own.astype(BF16), NT, preferred_element_type=F32
    )

    wide = min(256, grows)

    def permute(mat, src, dst, which):
        data = src[which].reshape(grows, HDIM)

        @pl.loop(0, grows // wide)
        def _(c):
            moved = jnp.dot(
                mat[pl.ds(c * wide, wide), :], data, preferred_element_type=F32
            ).astype(BF16)
            dst[which, pl.ds(c * (wide // TILE), wide // TILE)] = moved.reshape(
                wide // TILE, TILE, HDIM
            )

    def hand_out(which, slot, phase):
        own[which, slot] = in2[which, me]

        @pl.loop(0, n_ctx - 1)
        def _(i):
            p = peer(i)
            send(in2.at[which, p], own.at[which, slot], phase, p)

    await_copy(in1.at[0, pl.ds(0, n_ctx - 1)], recv_sem.at[IN_A])
    permute(sort_mat, in1, in2, 0)
    hand_out(0, me, OWN_A)
    await_copy(in1.at[1, pl.ds(0, n_ctx - 1)], recv_sem.at[IN_B])
    permute(sort_mat, in1, in2, 1)

    @pl.when(half(me) == 1)
    def _():
        hand_out(1, pairs + half_tile(me), OWN_G)

    await_copy(own.at[0, pl.ds(0, n_ctx - 1)], recv_sem.at[OWN_A])
    q_own = own[0, pl.ds(0, pairs)].reshape(rows, HDIM)
    k_own = own[0, pl.ds(pairs, pairs)].reshape(rows, HDIM)
    part = min(256, rows)

    for c in range(rows // part):
        cut = slice(c * part, (c + 1) * part)
        scores = (
            lax.dot_general(k_own, q_own[cut], NT, preferred_element_type=F32) * scale
        )
        key_pos = piece_row(iota((rows, part), 0), block_rows)
        query_pos = piece_row(iota((rows, part), 1) + c * part, block_rows)
        allowed = (lanes(id_own, part)[:, :part] == id_own_lane[0:1, cut]) & (key_pos <= query_pos)
        scores = jnp.where(allowed, scores, -jnp.inf)
        exponent = jnp.exp(scores - jnp.max(scores, axis=0, keepdims=True))
        probs[:, cut] = exponent * (1.0 / jnp.sum(exponent, axis=0, keepdims=True))

    @pl.when(half(me) == 0)
    def _():
        hand_out(1, half_tile(me), OWN_V)

    local = (id_own_lane - (CLUS_DEV * me).astype(F32)) == iota((8, rows), 0).astype(F32)
    cen_buf[head] = jnp.dot(onehot(local), k_own, preferred_element_type=F32)

    @pl.loop(1, n_head)
    def _(i):
        send_head(cen_buf.at[head], cen_buf.at[head], CEN, (head + i) % n_head)

    k_t[...] = k_own.astype(F32).T.astype(BF16)

    def await_half(first, remote, sem):
        @pl.when(half(me) == remote)
        def _():
            await_copy(own.at[1, pl.ds(first, pairs)], sem)

        @pl.when(half(me) == 1 - remote)
        def _():
            await_copy(own.at[1, pl.ds(first, pairs - 1)], sem)

    probs_low[...] = probs[...].astype(BF16)
    await_half(pairs, 0, recv_sem.at[OWN_G])
    g_own = own[1, pl.ds(pairs, pairs)].reshape(rows, HDIM)

    values_grad = jnp.dot(probs_low[...], g_own, preferred_element_type=F32)
    res[pl.ds(2 * pairs, pairs)] = values_grad.astype(BF16).reshape(pairs, TILE, HDIM)

    @pl.when(half(me) == 1)
    def _():
        mid1[1, me] = res[2 * pairs + half_tile(me)]

    @pl.loop(0, n_ctx - 1)
    def _(i):
        p = peer(i)

        @pl.when(half(p) == 1)
        def _():
            send(res.at[2 * pairs + half_tile(p)], mid1.at[1, me], GV, p)

    await_half(0, 1, recv_sem.at[OWN_V])
    v_own = own[1, pl.ds(0, pairs)].reshape(rows, HDIM)

    for c in range(rows // part):
        cut = slice(c * part, (c + 1) * part)
        dprob = lax.dot_general(v_own, g_own[cut], NT, preferred_element_type=F32)
        prob = probs[:, cut]
        delta = jnp.sum(probs_low[:, cut].astype(F32) * dprob, axis=0, keepdims=True)
        dscore[:, cut] = (prob * (dprob - delta)).astype(BF16)

    keys_grad = jnp.dot(dscore[...], q_own, preferred_element_type=F32) * scale
    res[pl.ds(pairs, pairs)] = keys_grad.astype(BF16).reshape(pairs, TILE, HDIM)
    queries_grad = jnp.dot(k_t[...], dscore[...], preferred_element_type=F32) * scale
    res[pl.ds(0, pairs)] = queries_grad.T.astype(BF16).reshape(pairs, TILE, HDIM)
    mid1[0, me] = res[me]

    @pl.loop(0, n_ctx - 1)
    def _(i):
        p = peer(i)
        send(res.at[p], mid1.at[0, me], GQK, p)

    @pl.when(half(me) == 1)
    def _():
        await_copy(mid1.at[1, pl.ds(0, n_ctx - 1)], recv_sem.at[GV])
        permute(unsort_mat, mid1, mid2, 1)
        back_v[half_tile(me)] = mid2[1, me]

        @pl.loop(0, n_ctx - 1)
        def _(i):
            p = peer(i)
            send(mid2.at[1, p], back_v.at[half_tile(me)], BACK_V, p)

    await_copy(mid1.at[0, pl.ds(0, n_ctx - 1)], recv_sem.at[GQK])
    permute(unsort_mat, mid1, mid2, 0)
    back[me] = mid2[0, me]

    @pl.loop(0, n_ctx - 1)
    def _(i):
        p = peer(i)
        send(mid2.at[0, p], back.at[me], BACK_QK, p)

    await_copy(cen_buf.at[pl.ds(0, n_head - 1)], recv_sem.at[CEN])
    whole = cen_buf[0]
    for h in range(1, n_head):
        whole = whole + cen_buf[h]
    centroids = whole / jnp.sqrt(jnp.mean(whole * whole, axis=1, keepdims=True) + 1e-06)
    cen_own[...] = centroids[:CLUS_DEV]
    store_cen = pltpu.make_async_copy(cen_own, cen_ref, load_sem.at[1])
    store_cen.start()

    @pl.when(half(me) == 1)
    def _():
        await_copy(back_v.at[pl.ds(0, pairs - 1)], recv_sem.at[BACK_V])
        await_copy(res.at[pl.ds(2 * pairs, pairs - 1)], send_sem.at[GV])
        await_copy(mid2.at[1, pl.ds(0, n_ctx - 1)], send_sem.at[BACK_V])

    @pl.when(half(me) == 0)
    def _():
        await_copy(back_v.at[pl.ds(0, pairs)], recv_sem.at[BACK_V])
        await_copy(res.at[pl.ds(2 * pairs, pairs)], send_sem.at[GV])

    unpack([back_v[...]], [dv_own])
    store_dv = pltpu.make_async_copy(dv_own, dv_ref, load_sem.at[2])
    store_dv.start()
    groups = n_ctx // n_head

    @pl.when(collects)
    def _():
        await_copy(ids_all.at[pl.ds(0, groups - 1)], send_sem.at[IDS])

        @pl.loop(1, n_head)
        def _(i):
            await_copy(ids_all, send_sem.at[SHARE])

    @pl.when(jnp.logical_not(collects))
    def _():
        await_copy(ids_all.at[pl.ds(0, groups)], send_sem.at[IDS])

    await_copy(pack.at[pl.ds(0, n_ctx - 1)], send_sem.at[IN_A])
    await_copy(pack.at[pl.ds(0, n_ctx - 1)], send_sem.at[IN_B])
    await_copy(in2.at[0, pl.ds(0, n_ctx - 1)], send_sem.at[OWN_A])
    await_copy(in2.at[1, pl.ds(0, n_ctx - 1)], send_sem.at[OWN_V + half(me)])
    await_copy(res.at[pl.ds(0, n_ctx - 1)], send_sem.at[GQK])
    await_copy(mid2.at[0, pl.ds(0, n_ctx - 1)], send_sem.at[BACK_QK])
    await_copy(cen_buf.at[pl.ds(0, n_head - 1)], send_sem.at[CEN])
    store_cen.wait()
    store_dv.wait()
    await_copy(back.at[pl.ds(0, n_ctx - 1)], recv_sem.at[BACK_QK])


def finish(back, dv_in, cen_in, dq_out, dk_out, dv_out, cen_out, tiles, grads, cen, load, store):
    pairs = back.shape[0] // 2
    loads = [
        pltpu.make_async_copy(back.at[pl.ds(0, pairs)], tiles.at[0], load.at[0]),
        pltpu.make_async_copy(back.at[pl.ds(pairs, pairs)], tiles.at[1], load.at[1]),
        pltpu.make_async_copy(dv_in, grads.at[2], load.at[2]),
        pltpu.make_async_copy(cen_in, cen, load.at[3]),
    ]
    stores = [
        pltpu.make_async_copy(grads.at[0], dq_out, store.at[0]),
        pltpu.make_async_copy(grads.at[1], dk_out, store.at[1]),
        pltpu.make_async_copy(grads.at[2], dv_out, store.at[2]),
        pltpu.make_async_copy(cen, cen_out, store.at[3]),
    ]
    for copy in loads:
        copy.start()
    loads[0].wait()
    loads[1].wait()
    unpack([tiles[0], tiles[1]], [grads.at[0], grads.at[1]])
    for a in range(4):
        if a > 1:
            loads[a].wait()
        stores[a].start()
    for copy in stores:
        copy.wait()


def shards(queries, keys, values, out_grad, cluster_ids):
    n_ctx, n_head = lax.axis_size("ctx"), lax.axis_size("head")
    rows = queries.shape[0]
    pairs, grows = n_ctx // 2, TILE * n_ctx
    vmem = pl.BlockSpec(memory_space=pltpu.VMEM)
    hbm = pl.BlockSpec(memory_space=pltpu.HBM)
    grad = jax.ShapeDtypeStruct((rows, HDIM), BF16)
    centroid = jax.ShapeDtypeStruct((CLUS_DEV, HDIM), F32)
    back, dv, cen = pl.pallas_call(
        functools.partial(kernel, n_ctx, n_head),
        out_shape=(jax.ShapeDtypeStruct((n_ctx, TILE, HDIM), BF16), grad, centroid),
        in_specs=[hbm] * 5,
        out_specs=(vmem, hbm, hbm),
        scratch_shapes=[
            pltpu.VMEM((4, rows, HDIM), BF16),
            pltpu.SMEM((BLOCKS,), jnp.int32),
            pltpu.VMEM((1, HDIM), F32),
            pltpu.VMEM((4 * pairs, TILE, HDIM), BF16),
            pltpu.VMEM((n_ctx, 1, HDIM), F32),
            pltpu.VMEM((grows, HDIM), F32),
            pltpu.VMEM((2, n_ctx, TILE, HDIM), BF16),
            pltpu.VMEM((2, n_ctx, TILE, HDIM), BF16),
            pltpu.VMEM((2, n_ctx, TILE, HDIM), BF16),
            pltpu.VMEM((3 * pairs, TILE, HDIM), BF16),
            pltpu.VMEM((2, n_ctx, TILE, HDIM), BF16),
            pltpu.VMEM((2, n_ctx, TILE, HDIM), BF16),
            pltpu.VMEM((pairs, TILE, HDIM), BF16),
            pltpu.VMEM((grows, grows), BF16),
            pltpu.VMEM((grows, grows), BF16),
            pltpu.VMEM((rows, rows), F32),
            pltpu.VMEM((rows, rows), BF16),
            pltpu.VMEM((rows, rows), BF16),
            pltpu.VMEM((HDIM, rows), BF16),
            pltpu.VMEM((n_head, 8, HDIM), F32),
            pltpu.VMEM((CLUS_DEV, HDIM), F32),
            pltpu.VMEM((rows, HDIM), BF16),
            pltpu.SemaphoreType.DMA((5,)),
            pltpu.SemaphoreType.DMA((12,)),
            pltpu.SemaphoreType.DMA((12,)),
        ],
        compiler_params=pltpu.CompilerParams(
            collective_id=0, has_side_effects=True
        ),
        name="routing_attention",
    )(queries, keys, values, out_grad, cluster_ids)
    return pl.pallas_call(
        finish,
        out_shape=(grad, grad, grad, centroid),
        in_specs=[hbm] * 3,
        out_specs=(hbm,) * 4,
        scratch_shapes=[
            pltpu.VMEM((2, pairs, TILE, HDIM), BF16),
            pltpu.VMEM((3, rows, HDIM), BF16),
            pltpu.VMEM((CLUS_DEV, HDIM), F32),
            pltpu.SemaphoreType.DMA((4,)),
            pltpu.SemaphoreType.DMA((4,)),
        ],
        name="finish",
    )(back, dv, cen)


def solution(mesh):
    placed = (P("ctx", "head"), P("ctx", "head"), P("ctx", "head"), P("ctx", "head"), P("ctx"))
    return jax.shard_map(
        shards,
        mesh=mesh,
        in_specs=placed,
        out_specs=(P("ctx", "head"), P("ctx", "head"), P("ctx", "head"), P("ctx", None)),
        check_vma=False,
    )
```

```python
import functools
import math

import jax
import jax.numpy as jnp
from jax import lax
from jax.experimental import pallas as pl
from jax.experimental.pallas import tpu as pltpu
from jax.sharding import PartitionSpec as P

HDIM = 128
CLUS_DEV = 4
BLOCKS = 8
TILE = 16
RING_Y = 4
MESH = pl.DeviceIdType.MESH
NT = (((1,), (1,)), ((), ()))
F32 = jnp.float32
BF16 = jnp.bfloat16

IDS, IN_A, IN_B, OWN_A, OWN_V, OWN_G, GV, GQK, BACK_V, BACK_QK, CEN, SHARE = range(12)


def iota(shape, dim):
    return lax.broadcasted_iota(jnp.int32, shape, dim)


def onehot(mask):
    return jnp.where(mask, 1.0, 0.0).astype(BF16)


def piece_row(r, block_rows):
    return ((r >> 1) & (BLOCKS - 1)) * block_rows + 2 * (r >> 4) + (r & 1)


def lanes(column, width):
    return jnp.concatenate([column] * (width // HDIM), axis=1) if width > HDIM else column


def unpack(tiles, outs):
    rows = tiles[0].shape[0] * TILE
    data = jnp.concatenate([t.reshape(rows, HDIM) for t in tiles], axis=1)
    chunk = min(256, rows)
    for c in range(rows // chunk):
        source = piece_row(iota((chunk, rows), 1), rows // BLOCKS)
        picked = jnp.dot(
            onehot(source == iota((chunk, rows), 0) + c * chunk), data,
            preferred_element_type=F32,
        ).astype(BF16)
        for a, out in enumerate(outs):
            out[pl.ds(c * chunk, chunk), :] = picked[:, a * HDIM : (a + 1) * HDIM]


def kernel(
    n_ctx, n_head,
    q_ref, k_ref, v_ref, g_ref, id_ref,
    back, dv_ref, cen_ref,
    staged, id_words, id_row, pack, ids_all, idc, in1, in2, own, res, mid1, mid2, back_v,
    sort_mat, unsort_mat, probs, probs_low, dscore, k_t, cen_buf, cen_own, dv_own, load_sem, send_sem, recv_sem,
):
    me = lax.axis_index("ctx")
    head = lax.axis_index("head")
    core = head % 2
    my_z, my_y = me // RING_Y, me % RING_Y
    n_z = n_ctx // RING_Y
    pairs = n_ctx // 2
    rows = BLOCKS * n_ctx
    grows = TILE * n_ctx
    block_rows = n_ctx
    scale = 1.0 / math.sqrt(HDIM)

    def peer(i):
        odd, step = lax.rem(i, 2), lax.div(i, 8)
        dz = n_z // 2 + step - odd * (2 * step + 1)
        dy = lax.div(i, 2) + 1
        return lax.rem(my_z + dz, n_z) * RING_Y + lax.rem(my_y + dy, RING_Y)

    def half_tile(p):
        return lax.div(p, 2 * RING_Y) * RING_Y + lax.rem(p, RING_Y)

    def half(p):
        return lax.rem(lax.div(p, RING_Y) + core + 1, 2)

    def send(src, dst, phase, p):
        pltpu.make_async_remote_copy(
            src_ref=src, dst_ref=dst, send_sem=send_sem.at[phase], recv_sem=recv_sem.at[phase],
            device_id={"ctx": p}, device_id_type=MESH,
        ).start()

    def send_head(src, dst, phase, h):
        pltpu.make_async_remote_copy(
            src_ref=src, dst_ref=dst, send_sem=send_sem.at[phase], recv_sem=recv_sem.at[phase],
            device_id={"head": h}, device_id_type=MESH,
        ).start()

    def await_copy(ref, sem):
        pltpu.make_async_copy(ref, ref, sem).wait()

    barrier = pltpu.get_barrier_semaphore()

    @pl.loop(0, n_ctx - 1)
    def _(i):
        pl.semaphore_signal(barrier, 1, device_id={"ctx": peer(i)}, device_id_type=MESH)

    @pl.loop(1, n_head)
    def _(i):
        pl.semaphore_signal(
            barrier, 1, device_id={"head": (head + i) % n_head}, device_id_type=MESH
        )

    loads = [
        pltpu.make_async_copy(ref, staged.at[a], load_sem.at[a])
        for a, ref in enumerate((q_ref, k_ref, v_ref, g_ref))
    ] + [pltpu.make_async_copy(id_ref, id_words, load_sem.at[4])]
    for load in loads:
        load.start()
    for a in (0, 1, 4):
        loads[a].wait()

    chunk = min(128, rows)

    def pack_two(first):
        every = jnp.concatenate([staged[first], staged[first + 1]], axis=1)

        @pl.loop(0, rows // chunk)
        def _(c):
            source = piece_row(iota((chunk, rows), 0) + c * chunk, block_rows)
            picked = jnp.dot(
                onehot(source == iota((chunk, rows), 1)), every, preferred_element_type=F32
            ).astype(BF16)
            tiles = chunk // TILE
            for a in range(2):
                pack[pl.ds((first + a) * pairs + c * tiles, tiles)] = picked[
                    :, a * HDIM : (a + 1) * HDIM
                ].reshape(tiles, TILE, HDIM)

    pack_two(0)
    words = jnp.zeros((1, HDIM), jnp.int32)
    for b in range(BLOCKS):
        words = jnp.where(iota((1, HDIM), 1) == b, id_words[b], words)
    id_row[...] = words.astype(F32)
    collects = me % n_head == head

    @pl.when(collects)
    def _():
        ids_all[me] = id_row[...]


    def second(p):
        return n_ctx + half(p) * pairs + half_tile(p)

    in1[0, me] = pack[me]

    pl.semaphore_wait(barrier, n_ctx - 1 + n_head - 1)

    @pl.loop(0, n_ctx // n_head)
    def _(i):
        p = i * n_head + head

        @pl.when(p != me)
        def _():
            send(id_row, ids_all.at[me], IDS, p)

    @pl.loop(0, n_ctx - 1)
    def _(i):
        p = peer(i)
        send(pack.at[p], in1.at[0, me], IN_A, p)

    loads[2].wait()
    loads[3].wait()
    pack_two(2)
    in1[1, me] = pack[second(me)]

    @pl.loop(0, n_ctx - 1)
    def _(i):
        p = peer(i)
        send(pack.at[second(p)], in1.at[1, me], IN_B, p)

    @pl.when(collects)
    def _():
        await_copy(ids_all.at[pl.ds(0, n_ctx - 1)], recv_sem.at[IDS])

        @pl.loop(1, n_head)
        def _(i):
            send_head(ids_all, ids_all, SHARE, (head + i) % n_head)

    @pl.when(jnp.logical_not(collects))
    def _():
        await_copy(ids_all, recv_sem.at[SHARE])

    id_rows = ids_all[...].reshape(n_ctx, HDIM).astype(BF16)
    spread = jnp.dot(
        onehot((iota((grows, n_ctx), 0) >> 4) == iota((grows, n_ctx), 1)),
        id_rows, preferred_element_type=F32,
    )
    keep = ((iota((grows, HDIM), 0) >> 1) & (BLOCKS - 1)) == iota((grows, HDIM), 1)
    spread = jnp.where(keep, spread, 0.0).astype(BF16)
    idc[...] = jnp.dot(spread, jnp.ones((HDIM, HDIM), BF16), preferred_element_type=F32)
    id_lane = lax.dot_general(jnp.ones((8, HDIM), BF16), spread, NT, preferred_element_type=F32)
    owner_lane = jnp.floor(id_lane[0:1] * (1.0 / CLUS_DEV))

    step = min(128, grows)

    def rank(c, before):
        owner = jnp.floor(idc[pl.ds(c * step, step), :] * (1.0 / CLUS_DEV))
        same = lanes(owner, grows) == owner_lane
        row = (iota((step, grows), 0) + c * step) >> 1
        column = iota((step, grows), 1) >> 1
        before = before + jnp.sum(
            jnp.where(same & (row < column), 1.0, 0.0), axis=0, keepdims=True
        )
        return before

    before = lax.fori_loop(0, grows // step, rank, jnp.zeros((1, grows), F32))
    place_lane = TILE * owner_lane + before + (iota((1, grows), 1) & 1).astype(F32)

    @pl.loop(0, grows // step)
    def _(c):
        row = (iota((step, grows), 0) + c * step).astype(F32)
        sort_mat[pl.ds(c * step, step), :] = onehot(row == place_lane)

    id_tile = jnp.dot(
        sort_mat[pl.ds(pl.multiple_of(me * TILE, TILE), TILE), :], idc[...].astype(BF16),
        preferred_element_type=F32,
    )
    id_own = jnp.concatenate([id_tile] * pairs, axis=0)
    id_own_lane = lax.dot_general(
        onehot(iota((8, HDIM), 1) == 0), id_own.astype(BF16), NT, preferred_element_type=F32
    )

    wide = min(256, grows)

    def permute(mat, src, dst, which):
        data = src[which].reshape(grows, HDIM)

        @pl.loop(0, grows // wide)
        def _(c):
            moved = jnp.dot(
                mat[pl.ds(c * wide, wide), :], data, preferred_element_type=F32
            ).astype(BF16)
            dst[which, pl.ds(c * (wide // TILE), wide // TILE)] = moved.reshape(
                wide // TILE, TILE, HDIM
            )

    def hand_out(which, slot, phase):
        own[which, slot] = in2[which, me]

        @pl.loop(0, n_ctx - 1)
        def _(i):
            p = peer(i)
            send(in2.at[which, p], own.at[which, slot], phase, p)

    await_copy(in1.at[0, pl.ds(0, n_ctx - 1)], recv_sem.at[IN_A])
    permute(sort_mat, in1, in2, 0)
    hand_out(0, me, OWN_A)

    @pl.loop(0, grows // step)
    def _(c):
        owner = jnp.floor(idc[pl.ds(c * step, step), :] * (1.0 / CLUS_DEV))
        same = lanes(owner, grows) == owner_lane
        row = (iota((step, grows), 0) + c * step) >> 1
        column = iota((step, grows), 1) >> 1
        ahead = jnp.dot(
            onehot(same & (column < row)), jnp.ones((grows, HDIM), BF16),
            preferred_element_type=F32,
        )
        parity = (iota((step, HDIM), 0) & 1).astype(F32)
        place = TILE * owner + ahead + parity
        unsort_mat[pl.ds(c * step, step), :] = onehot(
            lanes(place, grows) == iota((step, grows), 1).astype(F32)
        )

    await_copy(in1.at[1, pl.ds(0, n_ctx - 1)], recv_sem.at[IN_B])
    permute(sort_mat, in1, in2, 1)

    @pl.when(half(me) == 1)
    def _():
        hand_out(1, pairs + half_tile(me), OWN_G)

    await_copy(own.at[0, pl.ds(0, n_ctx - 1)], recv_sem.at[OWN_A])
    q_own = own[0, pl.ds(0, pairs)].reshape(rows, HDIM)
    k_own = own[0, pl.ds(pairs, pairs)].reshape(rows, HDIM)
    part = min(256, rows)

    for c in range(rows // part):
        cut = slice(c * part, (c + 1) * part)
        scores = (
            lax.dot_general(k_own, q_own[cut], NT, preferred_element_type=F32) * scale
        )
        key_pos = piece_row(iota((rows, part), 0), block_rows)
        query_pos = piece_row(iota((rows, part), 1) + c * part, block_rows)
        allowed = (lanes(id_own, part)[:, :part] == id_own_lane[0:1, cut]) & (key_pos <= query_pos)
        scores = jnp.where(allowed, scores, -jnp.inf)
        exponent = jnp.exp(scores - jnp.max(scores, axis=0, keepdims=True))
        probs[:, cut] = exponent * (1.0 / jnp.sum(exponent, axis=0, keepdims=True))

    @pl.when(half(me) == 0)
    def _():
        hand_out(1, half_tile(me), OWN_V)

    local = (id_own_lane - (CLUS_DEV * me).astype(F32)) == iota((8, rows), 0).astype(F32)
    cen_buf[head] = jnp.dot(onehot(local), k_own, preferred_element_type=F32)

    @pl.loop(1, n_head)
    def _(i):
        send_head(cen_buf.at[head], cen_buf.at[head], CEN, (head + i) % n_head)

    k_t[...] = k_own.astype(F32).T.astype(BF16)

    def await_half(first, remote, sem):
        @pl.when(half(me) == remote)
        def _():
            await_copy(own.at[1, pl.ds(first, pairs)], sem)

        @pl.when(half(me) == 1 - remote)
        def _():
            await_copy(own.at[1, pl.ds(first, pairs - 1)], sem)

    probs_low[...] = probs[...].astype(BF16)
    await_half(pairs, 0, recv_sem.at[OWN_G])
    g_own = own[1, pl.ds(pairs, pairs)].reshape(rows, HDIM)

    values_grad = jnp.dot(probs_low[...], g_own, preferred_element_type=F32)
    res[pl.ds(2 * pairs, pairs)] = values_grad.astype(BF16).reshape(pairs, TILE, HDIM)

    @pl.when(half(me) == 1)
    def _():
        mid1[1, me] = res[2 * pairs + half_tile(me)]

    @pl.loop(0, n_ctx - 1)
    def _(i):
        p = peer(i)

        @pl.when(half(p) == 1)
        def _():
            send(res.at[2 * pairs + half_tile(p)], mid1.at[1, me], GV, p)

    await_half(0, 1, recv_sem.at[OWN_V])
    v_own = own[1, pl.ds(0, pairs)].reshape(rows, HDIM)

    for c in range(rows // part):
        cut = slice(c * part, (c + 1) * part)
        dprob = lax.dot_general(v_own, g_own[cut], NT, preferred_element_type=F32)
        prob = probs[:, cut]
        delta = jnp.sum(probs_low[:, cut].astype(F32) * dprob, axis=0, keepdims=True)
        dscore[:, cut] = (prob * (dprob - delta)).astype(BF16)

    keys_grad = jnp.dot(dscore[...], q_own, preferred_element_type=F32) * scale
    res[pl.ds(pairs, pairs)] = keys_grad.astype(BF16).reshape(pairs, TILE, HDIM)
    queries_grad = jnp.dot(k_t[...], dscore[...], preferred_element_type=F32) * scale
    res[pl.ds(0, pairs)] = queries_grad.T.astype(BF16).reshape(pairs, TILE, HDIM)
    mid1[0, me] = res[me]

    @pl.loop(0, n_ctx - 1)
    def _(i):
        p = peer(i)
        send(res.at[p], mid1.at[0, me], GQK, p)

    @pl.when(half(me) == 1)
    def _():
        await_copy(mid1.at[1, pl.ds(0, n_ctx - 1)], recv_sem.at[GV])
        permute(unsort_mat, mid1, mid2, 1)
        back_v[half_tile(me)] = mid2[1, me]

        @pl.loop(0, n_ctx - 1)
        def _(i):
            p = peer(i)
            send(mid2.at[1, p], back_v.at[half_tile(me)], BACK_V, p)

    await_copy(mid1.at[0, pl.ds(0, n_ctx - 1)], recv_sem.at[GQK])
    permute(unsort_mat, mid1, mid2, 0)
    back[me] = mid2[0, me]

    @pl.loop(0, n_ctx - 1)
    def _(i):
        p = peer(i)
        send(mid2.at[0, p], back.at[me], BACK_QK, p)

    await_copy(cen_buf.at[pl.ds(0, n_head - 1)], recv_sem.at[CEN])
    whole = cen_buf[0]
    for h in range(1, n_head):
        whole = whole + cen_buf[h]
    centroids = whole / jnp.sqrt(jnp.mean(whole * whole, axis=1, keepdims=True) + 1e-06)
    cen_own[...] = centroids[:CLUS_DEV]
    store_cen = pltpu.make_async_copy(cen_own, cen_ref, load_sem.at[1])
    store_cen.start()

    @pl.when(half(me) == 1)
    def _():
        await_copy(back_v.at[pl.ds(0, pairs - 1)], recv_sem.at[BACK_V])
        await_copy(res.at[pl.ds(2 * pairs, pairs - 1)], send_sem.at[GV])
        await_copy(mid2.at[1, pl.ds(0, n_ctx - 1)], send_sem.at[BACK_V])

    @pl.when(half(me) == 0)
    def _():
        await_copy(back_v.at[pl.ds(0, pairs)], recv_sem.at[BACK_V])
        await_copy(res.at[pl.ds(2 * pairs, pairs)], send_sem.at[GV])

    unpack([back_v[...]], [dv_own])
    store_dv = pltpu.make_async_copy(dv_own, dv_ref, load_sem.at[2])
    store_dv.start()
    groups = n_ctx // n_head

    @pl.when(collects)
    def _():
        await_copy(ids_all.at[pl.ds(0, groups - 1)], send_sem.at[IDS])

        @pl.loop(1, n_head)
        def _(i):
            await_copy(ids_all, send_sem.at[SHARE])

    @pl.when(jnp.logical_not(collects))
    def _():
        await_copy(ids_all.at[pl.ds(0, groups)], send_sem.at[IDS])

    await_copy(pack.at[pl.ds(0, n_ctx - 1)], send_sem.at[IN_A])
    await_copy(pack.at[pl.ds(0, n_ctx - 1)], send_sem.at[IN_B])
    await_copy(in2.at[0, pl.ds(0, n_ctx - 1)], send_sem.at[OWN_A])
    await_copy(in2.at[1, pl.ds(0, n_ctx - 1)], send_sem.at[OWN_V + half(me)])
    await_copy(res.at[pl.ds(0, n_ctx - 1)], send_sem.at[GQK])
    await_copy(mid2.at[0, pl.ds(0, n_ctx - 1)], send_sem.at[BACK_QK])
    await_copy(cen_buf.at[pl.ds(0, n_head - 1)], send_sem.at[CEN])
    store_cen.wait()
    store_dv.wait()
    await_copy(back.at[pl.ds(0, n_ctx - 1)], recv_sem.at[BACK_QK])


def finish(back, dv_in, cen_in, dq_out, dk_out, dv_out, cen_out, tiles, grads, cen, load, store):
    pairs = back.shape[0] // 2
    loads = [
        pltpu.make_async_copy(back.at[pl.ds(0, pairs)], tiles.at[0], load.at[0]),
        pltpu.make_async_copy(back.at[pl.ds(pairs, pairs)], tiles.at[1], load.at[1]),
        pltpu.make_async_copy(dv_in, grads.at[2], load.at[2]),
        pltpu.make_async_copy(cen_in, cen, load.at[3]),
    ]
    stores = [
        pltpu.make_async_copy(grads.at[0], dq_out, store.at[0]),
        pltpu.make_async_copy(grads.at[1], dk_out, store.at[1]),
        pltpu.make_async_copy(grads.at[2], dv_out, store.at[2]),
        pltpu.make_async_copy(cen, cen_out, store.at[3]),
    ]
    for copy in loads:
        copy.start()
    loads[0].wait()
    loads[1].wait()
    unpack([tiles[0], tiles[1]], [grads.at[0], grads.at[1]])
    for a in range(4):
        if a > 1:
            loads[a].wait()
        stores[a].start()
    for copy in stores:
        copy.wait()


def shards(queries, keys, values, out_grad, cluster_ids):
    n_ctx, n_head = lax.axis_size("ctx"), lax.axis_size("head")
    rows = queries.shape[0]
    pairs, grows = n_ctx // 2, TILE * n_ctx
    vmem = pl.BlockSpec(memory_space=pltpu.VMEM)
    hbm = pl.BlockSpec(memory_space=pltpu.HBM)
    grad = jax.ShapeDtypeStruct((rows, HDIM), BF16)
    centroid = jax.ShapeDtypeStruct((CLUS_DEV, HDIM), F32)
    back, dv, cen = pl.pallas_call(
        functools.partial(kernel, n_ctx, n_head),
        out_shape=(jax.ShapeDtypeStruct((n_ctx, TILE, HDIM), BF16), grad, centroid),
        in_specs=[hbm] * 5,
        out_specs=(vmem, hbm, hbm),
        scratch_shapes=[
            pltpu.VMEM((4, rows, HDIM), BF16),
            pltpu.SMEM((BLOCKS,), jnp.int32),
            pltpu.VMEM((1, HDIM), F32),
            pltpu.VMEM((4 * pairs, TILE, HDIM), BF16),
            pltpu.VMEM((n_ctx, 1, HDIM), F32),
            pltpu.VMEM((grows, HDIM), F32),
            pltpu.VMEM((2, n_ctx, TILE, HDIM), BF16),
            pltpu.VMEM((2, n_ctx, TILE, HDIM), BF16),
            pltpu.VMEM((2, n_ctx, TILE, HDIM), BF16),
            pltpu.VMEM((3 * pairs, TILE, HDIM), BF16),
            pltpu.VMEM((2, n_ctx, TILE, HDIM), BF16),
            pltpu.VMEM((2, n_ctx, TILE, HDIM), BF16),
            pltpu.VMEM((pairs, TILE, HDIM), BF16),
            pltpu.VMEM((grows, grows), BF16),
            pltpu.VMEM((grows, grows), BF16),
            pltpu.VMEM((rows, rows), F32),
            pltpu.VMEM((rows, rows), BF16),
            pltpu.VMEM((rows, rows), BF16),
            pltpu.VMEM((HDIM, rows), BF16),
            pltpu.VMEM((n_head, 8, HDIM), F32),
            pltpu.VMEM((CLUS_DEV, HDIM), F32),
            pltpu.VMEM((rows, HDIM), BF16),
            pltpu.SemaphoreType.DMA((5,)),
            pltpu.SemaphoreType.DMA((12,)),
            pltpu.SemaphoreType.DMA((12,)),
        ],
        compiler_params=pltpu.CompilerParams(
            collective_id=0, has_side_effects=True
        ),
        name="routing_attention",
    )(queries, keys, values, out_grad, cluster_ids)
    return pl.pallas_call(
        finish,
        out_shape=(grad, grad, grad, centroid),
        in_specs=[hbm] * 3,
        out_specs=(hbm,) * 4,
        scratch_shapes=[
            pltpu.VMEM((2, pairs, TILE, HDIM), BF16),
            pltpu.VMEM((3, rows, HDIM), BF16),
            pltpu.VMEM((CLUS_DEV, HDIM), F32),
            pltpu.SemaphoreType.DMA((4,)),
            pltpu.SemaphoreType.DMA((4,)),
        ],
        name="finish",
    )(back, dv, cen)


def solution(mesh):
    placed = (P("ctx", "head"), P("ctx", "head"), P("ctx", "head"), P("ctx", "head"), P("ctx"))
    return jax.shard_map(
        shards,
        mesh=mesh,
        in_specs=placed,
        out_specs=(P("ctx", "head"), P("ctx", "head"), P("ctx", "head"), P("ctx", None)),
        check_vma=False,
    )
```
